128 devices in a mesh: dom: 32 (over z, x, core), feat: 4 (over y).
Axes of the slice: x: 4, y: 4, z: 4, core: 2. Of those that a mesh axis runs over, the one named last changes fastest.
Arguments:
- feats: bfloat16 [65536, 768], P('dom', 'feat'), may hold values from -6 to 6
- tile_vals: bfloat16 [6144, 128, 128], P('dom'), may hold values from 0 to 1
- tile_dst: int32 [6144], P('dom'), may hold values from 0 to 15
- tile_src: int32 [6144], P('dom'), may hold values from 0 to 79
- tile_count: int32 [32], P('dom'), may hold values from 96 to 192, as said below
- send_blocks: int32 [32, 8, 8], P('dom'), may hold values from 0 to 15
- send_count: int32 [32, 8], P('dom'), may hold values from 1 to 8, as said below
- w_self: bfloat16 [3, 768, 768], replicated, may hold values from -0.21875 to 0.21875
- w_nbr: bfloat16 [3, 768, 768], replicated, may hold values from -0.21875 to 0.21875
- bias: float32 [3, 768], replicated, may hold values from -3 to 3
Outputs:
- hidden: bfloat16 [65536, 768], P('dom', 'feat')
The draws below stay inside these ranges and needn't reach their ends.
Inputs may be any that keep to these rules, and one draw needn't show every extreme that they name: `tile_count`: some partition has exactly 192 live tiles. `send_count`: some partition sends exactly 8 blocks to some peer.
All inputs are finite; a program needn't handle non-finite values.
Results may differ from the reference program's by a relative error of at most 0.0085.
Values may be sent and summed in bfloat16 or wider, within the bound.
A program may use at most 128 MiB of HBM per device.

```python
import jax
import jax.numpy as jnp
from jax import lax

D = 768
LAYERS = 3
BLK = 128
PEERS = 8
NODE_DEV = 2048
TILES_DEV = 192
SLOTS = 8
BLK_DEV = 16
NODES = 65536
TILES = 6144
SRCS = 80
N_DOM = 32


def draw_tile_vals(key, part):
    first, second, third = jax.random.split(jax.random.fold_in(key, 11), 3)
    picks = jax.random.uniform(first, (TILES, BLK, BLK), jnp.float32)
    present = (picks < 3.0 / BLK).astype(jnp.float32)
    diag_mask = jnp.eye(BLK, dtype=jnp.float32)[None, :, :]
    entries = jax.random.uniform(second, (TILES, BLK, BLK), jnp.float32, 0.25, 1.0)
    diag_vals = jax.random.uniform(third, (TILES, BLK, BLK), jnp.float32, 0.5, 1.0)
    off_part = entries * present * (1.0 - diag_mask)
    return (off_part + diag_vals * diag_mask).astype(jnp.bfloat16)


def draw_tile_count(key, part):
    first, second = jax.random.split(key)
    parts_total = TILES // TILES_DEV
    counts = jax.random.randint(first, (parts_total,), TILES_DEV // 2, TILES_DEV + 1)
    where = jax.random.randint(second, (), 0, parts_total)
    return counts.at[where].set(TILES_DEV).astype(jnp.int32)


def draw_send_count(key, part):
    first, second = jax.random.split(jax.random.fold_in(key, 7))
    parts_total = NODES // NODE_DEV
    counts = jax.random.randint(first, (parts_total * PEERS,), 1, SLOTS + 1)
    where = jax.random.randint(second, (), 0, parts_total * PEERS)
    return counts.at[where].set(SLOTS).reshape(parts_total, PEERS).astype(jnp.int32)


def touch_ends(drawn, rng, low, high):
    dims = drawn.shape
    spot = [jax.random.randint(jax.random.fold_in(rng, axis), (), 0, dims[axis]) for axis in range(len(dims))]
    drawn = drawn.at[tuple(spot)].set(low)
    longest = dims.index(max(dims))
    spot[longest] = (spot[longest] + 1) % dims[longest]
    return drawn.at[tuple(spot)].set(high)


def block_scale(key, dims, cuts, low, top_value):
    def one(position, parts):
        draws = jax.random.uniform(jax.random.fold_in(jax.random.fold_in(key, 6), position), (parts,), jnp.float32, low / len(cuts), top_value / len(cuts))
        return jnp.repeat(jnp.exp(draws), dims[position] // parts).reshape((-1,) + (1,) * (len(dims) - position - 1))

    gain = one(*cuts[0])
    for cut in cuts[1:]:
        gain = gain * one(*cut)
    return gain


def scatter_about(rng, dims, deviation, most, cuts=(), kind=jnp.bfloat16):
    result = deviation * jax.random.normal(rng, dims, jnp.float32)
    if cuts:
        result = result * block_scale(rng, dims, cuts, -0.22, 0.18)
    return jnp.clip(result, -most, most).astype(kind)


def setup_inputs(seed: int = 0) -> dict:
    splits = jax.random.split(jax.random.key(seed), 11)
    feats = scatter_about(splits[0], (NODES, D), 1.0, 6.0, ((0, 32), (1, 4)))
    tile_vals = draw_tile_vals(jax.random.fold_in(splits[10], 71), 0)
    tile_dst = touch_ends(jax.random.randint(splits[2], (TILES,), 0, BLK_DEV), jax.random.fold_in(splits[2], 1), 0, BLK_DEV - 1).astype(jnp.int32)
    tile_src = touch_ends(jax.random.randint(splits[3], (TILES,), 0, SRCS), jax.random.fold_in(splits[3], 1), 0, SRCS - 1).astype(jnp.int32)
    tile_count = draw_tile_count(jax.random.fold_in(splits[10], 71), 0)
    send_blocks = touch_ends(jax.random.randint(splits[5], (N_DOM, PEERS, SLOTS), 0, BLK_DEV), jax.random.fold_in(splits[5], 1), 0, BLK_DEV - 1).astype(jnp.int32)
    send_count = draw_send_count(jax.random.fold_in(splits[10], 71), 0)
    w_self = scatter_about(splits[7], (LAYERS, D, D), D ** -0.5, 0.21875)
    w_nbr = scatter_about(splits[8], (LAYERS, D, D), D ** -0.5, 0.21875)
    bias = scatter_about(splits[9], (LAYERS, D), 0.5, 3.0, (), jnp.float32)
    return dict(feats=feats, tile_vals=tile_vals, tile_dst=tile_dst, tile_src=tile_src, tile_count=tile_count, send_blocks=send_blocks, send_count=send_count, w_self=w_self, w_nbr=w_nbr, bias=bias)


def reference(feats, tile_vals, tile_dst, tile_src, tile_count, send_blocks, send_count, w_self, w_nbr, bias):
    nparts = N_DOM
    blk_dev = NODE_DEV // BLK
    offsets = jnp.array([(d // 2 + 1) * (1 if d % 2 == 0 else -1) for d in range(PEERS)], jnp.int32)
    peer_ids = jnp.arange(PEERS, dtype=jnp.int32)
    values = tile_vals.reshape(nparts, TILES_DEV, BLK, BLK)
    dst_ids = tile_dst.reshape(nparts, TILES_DEV)
    src_ids = tile_src.reshape(nparts, TILES_DEV)
    live = jnp.arange(TILES_DEV, dtype=jnp.int32)[None, :] < tile_count[:, None]
    masked = values * live[:, :, None, None].astype(jnp.bfloat16)
    onehot = (dst_ids[:, None, :] == jnp.arange(blk_dev, dtype=jnp.int32)[None, :, None]).astype(jnp.float32)
    row_sums = jnp.sum(masked.astype(jnp.float32), axis=3)
    degree = 1.0 + jnp.einsum('nbt,nti->nbi', onehot, row_sums)
    hidden = feats
    for layer in range(LAYERS):
        blocks_all = hidden.reshape(nparts, blk_dev, BLK, D)

        def aggregate(part):
            sources = (part - offsets) % nparts
            chosen = send_blocks[sources, peer_ids]
            filled = jnp.arange(SLOTS, dtype=jnp.int32)[None, :] < send_count[sources, peer_ids][:, None]
            received = blocks_all[sources[:, None], chosen] * filled[:, :, None, None].astype(jnp.bfloat16)
            source_list = jnp.concatenate([blocks_all[part], received.reshape(PEERS * SLOTS, BLK, D)], axis=0)
            picked = source_list[src_ids[part]]
            contrib = jnp.einsum('tij,tjf->tif', masked[part].astype(jnp.float32), picked.astype(jnp.float32))
            summed = jnp.einsum('bt,tif->bif', onehot[part], contrib)
            return (summed / degree[part][:, :, None]).astype(jnp.bfloat16)

        agg = lax.map(aggregate, jnp.arange(nparts, dtype=jnp.int32)).reshape(NODES, D)
        pre = jnp.dot(hidden, w_self[layer], preferred_element_type=jnp.float32)
        pre = pre + jnp.dot(agg, w_nbr[layer], preferred_element_type=jnp.float32) + bias[layer][None, :]
        if layer < LAYERS - 1:
            pre = jax.nn.relu(pre)
        hidden = pre.astype(jnp.bfloat16)
    return hidden
```

```python
import functools

import jax
import jax.numpy as jnp
from jax import lax
from jax.experimental import pallas as pl
from jax.experimental.pallas import tpu as pltpu
from jax.sharding import PartitionSpec as P

LAYERS = 3
BLK = 128
PEERS = 8
SLOTS = 8
MESH = pl.DeviceIdType.MESH
LANES = 128
PACK = 192
HEAD = 16
NC = 4
PLACES = 9
VMEM_BYTES = 60 * 1024 * 1024


def offset(d):
    return (d // 2 + 1) * (1 if d % 2 == 0 else -1)


def exchange(h_ref, tab_ref, w_ref, b_ref, g_ref, s_ref, held, own, lhs, load_sem, keep_sem, tab_sem,
             ysend, yrecv, xsend, xrecv, psend, precv):
    i = lax.axis_index("dom")
    y = lax.axis_index("feat")
    n_dom = lax.axis_size("dom")
    core = lax.rem(i, 2)
    y_up, y_down = lax.rem(y + 1, 4), lax.rem(y + 3, 4)
    x_up, x_down = lax.rem(i + 2, n_dom), lax.rem(i + n_dom - 2, n_dom)
    partner = i + 1 - 2 * core
    rows = h_ref.shape[0] // NC
    half = rows // 2
    blocks = rows // PACK

    def hrows(n, part=None):
        if part is None:
            return pl.ds(n * rows, rows)
        return pl.ds(n * rows + part * half, half)

    def grows(n):
        return pl.ds(0, HEAD + rows) if n == 0 else pl.ds(HEAD + n * rows, rows)

    def remote(src, dst, send, recv, dom, feat):
        return pltpu.make_async_remote_copy(
            src_ref=src, dst_ref=dst, send_sem=send, recv_sem=recv,
            device_id=(dom, feat), device_id_type=MESH)

    loads = [pltpu.make_async_copy(h_ref.at[hrows(n)], held.at[y, hrows(n)], load_sem.at[n]) for n in range(NC)]
    for load in loads:
        load.start()
    tab_load = pltpu.make_async_copy(tab_ref, own.at[pl.ds(0, HEAD)], tab_sem)
    tab_load.start()

    barrier = pltpu.get_barrier_semaphore()
    for dom, feat in ((i, y_up), (i, y_down), (x_up, y), (x_down, y), (partner, y)):
        pl.semaphore_signal(barrier, inc=1, device_id=(dom, feat), device_id_type=MESH)
    pl.semaphore_wait(barrier, 5)

    sent = []
    up, down = [], []
    for n in range(NC):
        loads[n].wait()
        a = remote(held.at[y, hrows(n)], held.at[y, hrows(n)], ysend.at[0, n], yrecv.at[0, n], i, y_up)
        b = remote(held.at[y, hrows(n)], held.at[y, hrows(n)], ysend.at[1, n], yrecv.at[1, n], i, y_down)
        a.start()
        b.start()
        up.append(a)
        down.append(b)
        sent += [a, b]

    def gather_relay(n):
        up[n].wait_recv()
        a = remote(held.at[y_down, hrows(n, 0)], held.at[y_down, hrows(n, 0)], ysend.at[2, n], yrecv.at[2, n], i, y_up)
        a.start()
        down[n].wait_recv()
        b = remote(held.at[y_up, hrows(n, 1)], held.at[y_up, hrows(n, 1)], ysend.at[3, n], yrecv.at[3, n], i, y_down)
        b.start()
        sent.extend([a, b])
        return a, b

    lane = lax.broadcasted_iota(jnp.int32, (64, LANES), 1)
    low = lane < 64

    def project(n):
        for j in range(blocks):
            base = n * rows + j * PACK
            out = slice(j * BLK, (j + 1) * BLK)
            top = slice(j * BLK, j * BLK + 64)
            bot = slice(j * BLK + 64, (j + 1) * BLK)
            for a in range(4):
                lhs[out, a * LANES:(a + 1) * LANES] = held[a, base:base + BLK, :]
            for pair in range(2):
                p0 = held[2 * pair, base + BLK:base + PACK, :]
                p1 = held[2 * pair + 1, base + BLK:base + PACK, :]
                cols = slice(512 + pair * LANES, 512 + (pair + 1) * LANES)
                lhs[top, cols] = jnp.concatenate([p0[:, :64], p1[:, :64]], axis=1)
                lhs[bot, cols] = jnp.concatenate([p0[:, 64:], p1[:, 64:]], axis=1)
        res = jnp.dot(lhs[...], w_ref[...], preferred_element_type=jnp.float32) + b_ref[...]
        for j in range(blocks):
            r0 = j * BLK
            base = n * rows + j * PACK
            own[HEAD + base:HEAD + base + BLK, :] = res[r0:r0 + BLK, :LANES].astype(jnp.bfloat16)
            s_ref[base:base + BLK, :] = res[r0:r0 + BLK, LANES:2 * LANES]
            top = res[r0:r0 + 64, 2 * LANES:]
            bot = res[r0 + 64:r0 + BLK, 2 * LANES:]
            own[HEAD + base + BLK:HEAD + base + PACK, :] = jnp.where(
                low, top, pltpu.roll(bot, 64, 1)).astype(jnp.bfloat16)
            s_ref[base + BLK:base + PACK, :] = jnp.where(low, pltpu.roll(top, 64, 1), bot)

    ours, first, second = [], [], []

    def send_own(n):
        src = own.at[grows(n)]
        keep = pltpu.make_async_copy(src, g_ref.at[4, grows(n)], keep_sem.at[n])
        a = remote(src, g_ref.at[2, grows(n)], xsend.at[0, n], xrecv.at[0, n], x_up, y)
        b = remote(src, g_ref.at[6, grows(n)], xsend.at[1, n], xrecv.at[1, n], x_down, y)
        c = remote(src, g_ref.at[3 + 2 * core, grows(n)], psend.at[0, n], precv.at[0, n], partner, y)
        for copy in (a, b, c, keep):
            copy.start()
        ours.append((a, b, c, keep))
        sent.extend([a, b, c])

    def relay_one(n):
        a, b, _, _ = ours[n]
        a.wait_recv()
        u = remote(g_ref.at[2, grows(n)], g_ref.at[0, grows(n)], xsend.at[2, n], xrecv.at[2, n], x_up, y)
        pu = remote(g_ref.at[2, grows(n)], g_ref.at[1 + 2 * core, grows(n)], psend.at[1, n], precv.at[1, n], partner, y)
        u.start()
        pu.start()
        b.wait_recv()
        v = remote(g_ref.at[6, grows(n)], g_ref.at[8, grows(n)], xsend.at[3, n], xrecv.at[3, n], x_down, y)
        pv = remote(g_ref.at[6, grows(n)], g_ref.at[5 + 2 * core, grows(n)], psend.at[2, n], precv.at[2, n], partner, y)
        v.start()
        pv.start()
        first.append((u, v, pu, pv))
        sent.extend([u, v, pu, pv])

    def relay_two(n):
        u, v, _, _ = first[n]
        u.wait_recv()
        v.wait_recv()
        c = remote(g_ref.at[8 - 8 * core, grows(n)], g_ref.at[7 - 6 * core, grows(n)], psend.at[3, n], precv.at[3, n],
                   partner, y)
        c.start()
        second.append(c)
        sent.append(c)

    tab_load.wait()
    for n in range(NC):
        a, b = gather_relay(n)
        a.wait_recv()
        b.wait_recv()
        project(n)
        send_own(n)
        if n >= 1:
            relay_one(n - 1)
        if n >= 2:
            relay_two(n - 2)
    relay_one(NC - 1)
    for n in range(max(NC - 2, 0), NC):
        relay_two(n)
    for n in range(NC):
        ours[n][2].wait_recv()
        first[n][2].wait_recv()
        first[n][3].wait_recv()
        second[n].wait_recv()
        ours[n][3].wait()
    for copy in sent:
        copy.wait_send()


def aggregate(last, tidx, roff, starts, g_ref, t_ref, s_ref, out_ref, gv, tv, g_sem, t_sem):
    slot_rows = g_ref.shape[1]
    tiles = t_ref.shape[0]
    groups = 4
    per = tiles // groups
    copies = [
        pltpu.make_async_copy(g_ref.at[p], gv.at[pl.ds(p * slot_rows, slot_rows)], g_sem.at[p])
        for p in range(PLACES)
    ] + [
        pltpu.make_async_copy(t_ref.at[pl.ds(k * per, per)], tv.at[pl.ds(k * per, per)], t_sem.at[k])
        for k in range(groups)
    ]
    for copy in copies:
        copy.start()
    gv[PLACES * slot_rows:PLACES * slot_rows + PACK, :] = jnp.zeros((PACK, LANES), jnp.bfloat16)
    tv[tiles] = jnp.zeros((BLK, BLK), jnp.bfloat16)
    for copy in copies:
        copy.wait()
    lane = lax.broadcasted_iota(jnp.int32, (64, LANES), 1)
    low = lane < 64
    ones = jnp.ones((64, 64), jnp.bfloat16)

    def source(q):
        row = pl.multiple_of(roff[q], 16)
        left = gv[pl.ds(row, BLK), :]
        pack = gv[pl.ds(row + BLK, 64), :]
        right = jnp.concatenate([
            jnp.concatenate([pack[:, :64], ones], axis=1),
            jnp.concatenate([pack[:, 64:], ones], axis=1),
        ], axis=0)
        return jnp.concatenate([left, right], axis=1)

    def block(b, carry):
        def pair(p, acc):
            q = 2 * p
            lhs = jnp.concatenate([tv[tidx[q]], tv[tidx[q + 1]]], axis=1)
            rhs = jnp.concatenate([source(q), source(q + 1)], axis=0)
            return acc + jnp.dot(lhs, rhs, preferred_element_type=jnp.float32)

        acc = lax.fori_loop(starts[b], starts[b + 1], pair, jnp.zeros((BLK, 2 * LANES), jnp.float32))
        scale = 1.0 / (1.0 + acc[:, PACK:PACK + 1])
        left = acc[:, :LANES] * scale
        right = acc[:, LANES:] * scale
        pack = jnp.where(low, right[:64], pltpu.roll(right[64:], 64, 1))
        base = pl.multiple_of(b * PACK, PACK)
        left = left + s_ref[pl.ds(base, BLK), :]
        pack = pack + s_ref[pl.ds(base + BLK, 64), :]
        if last:
            row = pl.multiple_of(b * BLK, BLK)
            out_ref[pl.ds(row, BLK), :LANES] = left.astype(jnp.bfloat16)
            out_ref[pl.ds(row, 64), LANES:] = pack[:, :64].astype(jnp.bfloat16)
            out_ref[pl.ds(row + 64, 64), LANES:] = pltpu.roll(pack, 64, 1)[:, :64].astype(jnp.bfloat16)
        else:
            out_ref[pl.ds(base, BLK), :] = jnp.maximum(left, 0.0).astype(jnp.bfloat16)
            out_ref[pl.ds(base + BLK, 64), :] = jnp.maximum(pack, 0.0).astype(jnp.bfloat16)
        return carry

    lax.fori_loop(0, s_ref.shape[0] // PACK, block, 0)


def per_device(
    feats, tile_vals, tile_dst, tile_src, tile_count, send_blocks, send_count, w_self, w_nbr, bias
):
    node_rows, cols = feats.shape
    blk_dev = node_rows // BLK
    packed_rows = blk_dev * PACK
    slot_rows = HEAD + packed_rows
    zero_row = PLACES * slot_rows
    tiles = tile_vals.shape[0]
    entries = tiles + blk_dev
    y = lax.axis_index("feat")
    i32 = jnp.int32

    def cut(w):
        here = lax.dynamic_slice_in_dim(w, y * cols, cols, 2)
        return here.reshape(LAYERS, 4, cols, cols)

    ws, wn = cut(w_self), cut(w_nbr)
    w = jnp.concatenate([wn[..., :128], ws[..., :128], wn[..., 128:], ws[..., 128:]], axis=3)
    w = jnp.concatenate(
        [w[:, :, :128].reshape(LAYERS, 512, 384), w[:, :, 128:].reshape(LAYERS, 256, 384)], axis=1
    )
    bias_here = lax.dynamic_slice_in_dim(bias, y * cols, cols, 1)
    b_all = jnp.concatenate(
        [jnp.zeros((LAYERS, 128)), bias_here[:, :128], jnp.zeros((LAYERS, 64)), bias_here[:, 128:]], axis=1
    ).astype(jnp.float32)[:, None, :]

    f3 = feats.reshape(blk_dev, BLK, cols)
    hidden = jnp.concatenate(
        [f3[..., :128], jnp.concatenate([f3[:, :64, 128:], f3[:, 64:, 128:]], axis=2)], axis=1
    ).reshape(packed_rows, LANES)

    table = jnp.zeros((HEAD, LANES), jnp.bfloat16)
    table = table.at[:PEERS, :SLOTS].set(send_blocks[0].astype(jnp.bfloat16))
    table = table.at[:PEERS, SLOTS].set(send_count[0].astype(jnp.bfloat16))

    ids = jnp.arange(tiles, dtype=i32)
    live = ids < tile_count[0]
    dsts = jnp.arange(blk_dev, dtype=i32)
    hits = (tile_dst[None, :] == dsts[:, None]) & live[None, :]
    pairs = (jnp.sum(hits.astype(i32), axis=1) + 1) // 2
    starts = jnp.sum(jnp.where(dsts[None, :] < jnp.arange(blk_dev + 1, dtype=i32)[:, None], pairs[None, :], 0), axis=1)
    before = jnp.sum(jnp.where(dsts[None, :] < tile_dst[:, None], pairs[None, :], 0), axis=1)
    rank = jnp.sum(
        ((tile_dst[None, :] == tile_dst[:, None]) & (ids[None, :] < ids[:, None])).astype(i32), axis=1
    )
    place = jnp.where(live, 2 * before + rank, -1)
    here = place[None, :] == jnp.arange(entries, dtype=i32)[:, None]
    tidx = jnp.sum(jnp.where(here, ids[None, :] - tiles, 0), axis=1) + tiles
    sidx = jnp.sum(jnp.where(here, tile_src[None, :] + 1, 0), axis=1) - 1

    exchange_call = pl.pallas_call(
        exchange,
        out_shape=(
            jax.ShapeDtypeStruct((PLACES, slot_rows, LANES), jnp.bfloat16),
            jax.ShapeDtypeStruct((packed_rows, LANES), jnp.float32),
        ),
        in_specs=[
            pl.BlockSpec(memory_space=pl.ANY),
            pl.BlockSpec(memory_space=pl.ANY),
            pl.BlockSpec(memory_space=pltpu.VMEM),
            pl.BlockSpec(memory_space=pltpu.VMEM),
        ],
        out_specs=(pl.BlockSpec(memory_space=pl.ANY), pl.BlockSpec(memory_space=pltpu.VMEM)),
        scratch_shapes=[
            pltpu.VMEM((4, packed_rows, LANES), jnp.bfloat16),
            pltpu.VMEM((slot_rows, LANES), jnp.bfloat16),
            pltpu.VMEM((node_rows // NC, 768), jnp.bfloat16),
            pltpu.SemaphoreType.DMA((NC,)),
            pltpu.SemaphoreType.DMA((NC,)),
            pltpu.SemaphoreType.DMA,
            pltpu.SemaphoreType.DMA((4, NC)),
            pltpu.SemaphoreType.DMA((4, NC)),
            pltpu.SemaphoreType.DMA((4, NC)),
            pltpu.SemaphoreType.DMA((4, NC)),
            pltpu.SemaphoreType.DMA((4, NC)),
            pltpu.SemaphoreType.DMA((4, NC)),
        ],
        compiler_params=pltpu.CompilerParams(
            collective_id=0, has_side_effects=True, vmem_limit_bytes=VMEM_BYTES
        ),
        name="exchange",
    )

    def aggregate_call(last):
        out = (node_rows, cols) if last else (packed_rows, LANES)
        return pl.pallas_call(
            functools.partial(aggregate, last),
            out_shape=jax.ShapeDtypeStruct(out, jnp.bfloat16),
            grid_spec=pltpu.PrefetchScalarGridSpec(
                num_scalar_prefetch=3,
                grid=(),
                in_specs=[
                    pl.BlockSpec(memory_space=pl.ANY),
                    pl.BlockSpec(memory_space=pl.ANY),
                    pl.BlockSpec(memory_space=pltpu.VMEM),
                ],
                out_specs=pl.BlockSpec(memory_space=pltpu.VMEM),
                scratch_shapes=[
                    pltpu.VMEM((zero_row + PACK, LANES), jnp.bfloat16),
                    pltpu.VMEM((tiles + 1, BLK, BLK), jnp.bfloat16),
                    pltpu.SemaphoreType.DMA((PLACES,)),
                    pltpu.SemaphoreType.DMA((4,)),
                ],
            ),
            compiler_params=pltpu.CompilerParams(vmem_limit_bytes=VMEM_BYTES),
            name="aggregate_last" if last else "aggregate",
        )

    roff = None
    for layer in range(LAYERS):
        g, s = exchange_call(hidden, table, w[layer], b_all[layer])
        if layer == 0:
            spots = [4 - offset(d) for d in range(PEERS)]
            pick = (jnp.arange(PLACES)[:, None] == jnp.array(spots)[None, :]).astype(jnp.float32)
            heads = jnp.sum(g[:, :PEERS, :16].astype(jnp.float32) * pick[:, :, None], axis=0).astype(i32)
            filled = jnp.arange(SLOTS, dtype=i32)[None, :] < heads[:, SLOTS:SLOTS + 1]
            spot_rows = jnp.array(spots, i32)[:, None] * slot_rows + HEAD
            theirs = jnp.where(filled, spot_rows + PACK * heads[:, :SLOTS], zero_row).reshape(-1)
            mine = 4 * slot_rows + HEAD + PACK * dsts
            rows = jnp.concatenate([mine, theirs])
            srcs = jnp.arange(rows.shape[0], dtype=i32)
            roff = jnp.sum(jnp.where(sidx[:, None] == srcs[None, :], rows[None, :] - zero_row, 0), axis=1) + zero_row
        hidden = aggregate_call(layer == LAYERS - 1)(tidx, roff, starts, g, tile_vals, s)
    return hidden


def solution(mesh):
    in_specs = (
        P("dom", "feat"),
        P("dom", None, None),
        P("dom"),
        P("dom"),
        P("dom"),
        P("dom", None, None),
        P("dom", None),
        P(),
        P(),
        P(),
    )
    out_specs = P("dom", "feat")
    return jax.shard_map(
        per_device, mesh=mesh, in_specs=in_specs, out_specs=out_specs, check_vma=False
    )
```

```python
import functools

import jax
import jax.numpy as jnp
from jax import lax
from jax.experimental import pallas as pl
from jax.experimental.pallas import tpu as pltpu
from jax.sharding import PartitionSpec as P

LAYERS = 3
BLK = 128
PEERS = 8
SLOTS = 8
MESH = pl.DeviceIdType.MESH
LANES = 128
PACK = 192
HEAD = 16
CHUNKS = (4, 4, 4, 4)
AHEAD = 1
PLACES = 9
UNROLL = 8
VMEM_BYTES = 60 * 1024 * 1024


def offset(d):
    return (d // 2 + 1) * (1 if d % 2 == 0 else -1)


def exchange(h_ref, tab_ref, w_ref, b_ref, g_ref, s_ref, held, own, lhs, load_sem, keep_sem, tab_sem,
             ysend, yrecv, xsend, xrecv, psend, precv):
    i = lax.axis_index("dom")
    y = lax.axis_index("feat")
    n_dom = lax.axis_size("dom")
    core = lax.rem(i, 2)
    y_up, y_down = lax.rem(y + 1, 4), lax.rem(y + 3, 4)
    x_up, x_down = lax.rem(i + 2, n_dom), lax.rem(i + n_dom - 2, n_dom)
    partner = i + 1 - 2 * core
    NC = len(CHUNKS)
    first_row = [sum(CHUNKS[:n]) * PACK for n in range(NC)]

    def hrows(n, part=None):
        size = CHUNKS[n] * PACK
        if part is None:
            return pl.ds(first_row[n], size)
        return pl.ds(first_row[n] + part * (size // 2), size // 2)

    def grows(n):
        size = CHUNKS[n] * PACK
        return pl.ds(0, HEAD + size) if n == 0 else pl.ds(HEAD + first_row[n], size)

    def remote(src, dst, send, recv, dom, feat):
        return pltpu.make_async_remote_copy(
            src_ref=src, dst_ref=dst, send_sem=send, recv_sem=recv,
            device_id=(dom, feat), device_id_type=MESH)

    loads = [pltpu.make_async_copy(h_ref.at[hrows(n)], held.at[y, hrows(n)], load_sem.at[n]) for n in range(NC)]
    for load in loads:
        load.start()
    tab_load = pltpu.make_async_copy(tab_ref, own.at[pl.ds(0, HEAD)], tab_sem)
    tab_load.start()

    barrier = pltpu.get_barrier_semaphore()
    for dom, feat in ((i, y_up), (i, y_down), (x_up, y), (x_down, y), (partner, y)):
        pl.semaphore_signal(barrier, inc=1, device_id=(dom, feat), device_id_type=MESH)
    pl.semaphore_wait(barrier, 5)

    sent = []
    up, down = [], []

    def gather_own(n):
        loads[n].wait()
        a = remote(held.at[y, hrows(n)], held.at[y, hrows(n)], ysend.at[0, n], yrecv.at[0, n], i, y_up)
        b = remote(held.at[y, hrows(n)], held.at[y, hrows(n)], ysend.at[1, n], yrecv.at[1, n], i, y_down)
        a.start()
        b.start()
        up.append(a)
        down.append(b)
        sent.extend([a, b])

    for n in range(min(AHEAD, NC)):
        gather_own(n)

    def gather_relay(n):
        up[n].wait_recv()
        a = remote(held.at[y_down, hrows(n, 0)], held.at[y_down, hrows(n, 0)], ysend.at[2, n], yrecv.at[2, n], i, y_up)
        a.start()
        down[n].wait_recv()
        b = remote(held.at[y_up, hrows(n, 1)], held.at[y_up, hrows(n, 1)], ysend.at[3, n], yrecv.at[3, n], i, y_down)
        b.start()
        sent.extend([a, b])
        if n + AHEAD < NC:
            gather_own(n + AHEAD)
        return a, b

    lane = lax.broadcasted_iota(jnp.int32, (64, LANES), 1)
    low = lane < 64

    def project(n):
        blocks = CHUNKS[n]
        for j in range(blocks):
            base = first_row[n] + j * PACK
            out = slice(j * BLK, (j + 1) * BLK)
            top = slice(j * BLK, j * BLK + 64)
            bot = slice(j * BLK + 64, (j + 1) * BLK)
            for a in range(4):
                lhs[out, a * LANES:(a + 1) * LANES] = held[a, base:base + BLK, :]
            for pair in range(2):
                p0 = held[2 * pair, base + BLK:base + PACK, :]
                p1 = held[2 * pair + 1, base + BLK:base + PACK, :]
                cols = slice(512 + pair * LANES, 512 + (pair + 1) * LANES)
                lhs[top, cols] = jnp.concatenate([p0[:, :64], p1[:, :64]], axis=1)
                lhs[bot, cols] = jnp.concatenate([p0[:, 64:], p1[:, 64:]], axis=1)
        res = jnp.dot(lhs[:blocks * BLK], w_ref[...], preferred_element_type=jnp.float32) + b_ref[...]
        for j in range(blocks):
            r0 = j * BLK
            base = first_row[n] + j * PACK
            own[HEAD + base:HEAD + base + BLK, :] = res[r0:r0 + BLK, :LANES].astype(jnp.bfloat16)
            s_ref[base:base + BLK, :] = res[r0:r0 + BLK, LANES:2 * LANES]
            top = res[r0:r0 + 64, 2 * LANES:]
            bot = res[r0 + 64:r0 + BLK, 2 * LANES:]
            own[HEAD + base + BLK:HEAD + base + PACK, :] = jnp.where(
                low, top, pltpu.roll(bot, 64, 1)).astype(jnp.bfloat16)
            s_ref[base + BLK:base + PACK, :] = jnp.where(low, pltpu.roll(top, 64, 1), bot)

    ours, first, second = [], [], []

    def send_own(n):
        src = own.at[grows(n)]
        keep = pltpu.make_async_copy(src, g_ref.at[4, grows(n)], keep_sem.at[n])
        a = remote(src, g_ref.at[2, grows(n)], xsend.at[0, n], xrecv.at[0, n], x_up, y)
        b = remote(src, g_ref.at[6, grows(n)], xsend.at[1, n], xrecv.at[1, n], x_down, y)
        c = remote(src, g_ref.at[3 + 2 * core, grows(n)], psend.at[0, n], precv.at[0, n], partner, y)
        for copy in (a, b, c, keep):
            copy.start()
        ours.append((a, b, c, keep))
        sent.extend([a, b, c])

    def relay_one(n):
        a, b, _, _ = ours[n]
        a.wait_recv()
        u = remote(g_ref.at[2, grows(n)], g_ref.at[0, grows(n)], xsend.at[2, n], xrecv.at[2, n], x_up, y)
        pu = remote(g_ref.at[2, grows(n)], g_ref.at[1 + 2 * core, grows(n)], psend.at[1, n], precv.at[1, n], partner, y)
        u.start()
        pu.start()
        b.wait_recv()
        v = remote(g_ref.at[6, grows(n)], g_ref.at[8, grows(n)], xsend.at[3, n], xrecv.at[3, n], x_down, y)
        pv = remote(g_ref.at[6, grows(n)], g_ref.at[5 + 2 * core, grows(n)], psend.at[2, n], precv.at[2, n], partner, y)
        v.start()
        pv.start()
        first.append((u, v, pu, pv))
        sent.extend([u, v, pu, pv])

    def relay_two(n):
        u, v, _, _ = first[n]
        u.wait_recv()
        v.wait_recv()
        c = remote(g_ref.at[8 - 8 * core, grows(n)], g_ref.at[7 - 6 * core, grows(n)], psend.at[3, n], precv.at[3, n],
                   partner, y)
        c.start()
        second.append(c)
        sent.append(c)

    tab_load.wait()
    for n in range(NC):
        a, b = gather_relay(n)
        a.wait_recv()
        b.wait_recv()
        project(n)
        send_own(n)
        if n >= 1:
            relay_one(n - 1)
        if n >= 2:
            relay_two(n - 2)
    relay_one(NC - 1)
    for n in range(max(NC - 2, 0), NC):
        relay_two(n)
    for n in range(NC):
        ours[n][2].wait_recv()
        first[n][2].wait_recv()
        first[n][3].wait_recv()
        second[n].wait_recv()
        ours[n][3].wait()
    for copy in sent:
        copy.wait_send()


def aggregate(last, tidx, roff, keep, ends, g_ref, t_ref, s_ref, out_ref, gv, tv, part, g_sem, t_sem):
    slot_rows = g_ref.shape[1]
    tiles = t_ref.shape[0]
    groups = 4
    per = tiles // groups
    copies = [
        pltpu.make_async_copy(g_ref.at[p], gv.at[pl.ds(p * slot_rows, slot_rows)], g_sem.at[p])
        for p in range(PLACES)
    ] + [
        pltpu.make_async_copy(t_ref.at[pl.ds(k * per, per)], tv.at[pl.ds(k * per, per)], t_sem.at[k])
        for k in range(groups)
    ]
    for copy in copies:
        copy.start()
    gv[PLACES * slot_rows:PLACES * slot_rows + PACK, :] = jnp.zeros((PACK, LANES), jnp.bfloat16)
    tv[tiles] = jnp.zeros((BLK, BLK), jnp.bfloat16)
    for copy in copies:
        copy.wait()
    lane = lax.broadcasted_iota(jnp.int32, (64, LANES), 1)
    low = lane < 64
    ones = jnp.ones((64, 64), jnp.bfloat16)

    def source(q):
        row = pl.multiple_of(roff[q], 16)
        left = gv[pl.ds(row, BLK), :]
        pack = gv[pl.ds(row + BLK, 64), :]
        right = jnp.concatenate([
            jnp.concatenate([pack[:, :64], ones], axis=1),
            jnp.concatenate([pack[:, 64:], ones], axis=1),
        ], axis=0)
        return jnp.concatenate([left, right], axis=1)

    def product(p):
        q = 2 * p
        lhs = jnp.concatenate([tv[tidx[q]], tv[tidx[q + 1]]], axis=1)
        rhs = jnp.concatenate([source(q), source(q + 1)], axis=0)
        return jnp.dot(lhs, rhs, preferred_element_type=jnp.float32)

    part[0] = jnp.zeros(part.shape[1:], jnp.float32)

    def step(g, carry):
        products = [product(g * UNROLL + u) for u in range(UNROLL)]
        for u in range(UNROLL):
            p = g * UNROLL + u
            part[p + 1] = part[p] * keep[p] + products[u]
        return carry

    lax.fori_loop(0, (part.shape[0] - 1) // UNROLL, step, 0)

    for b in range(s_ref.shape[0] // PACK):
        acc = part[ends[b]]
        scale = 1.0 / (1.0 + acc[:, PACK:PACK + 1])
        left = acc[:, :LANES] * scale
        right = acc[:, LANES:] * scale
        pack = jnp.where(low, right[:64], pltpu.roll(right[64:], 64, 1))
        base = b * PACK
        left = left + s_ref[base:base + BLK, :]
        pack = pack + s_ref[base + BLK:base + PACK, :]
        if last:
            row = b * BLK
            out_ref[row:row + BLK, :LANES] = left.astype(jnp.bfloat16)
            out_ref[row:row + 64, LANES:] = pack[:, :64].astype(jnp.bfloat16)
            out_ref[row + 64:row + BLK, LANES:] = pltpu.roll(pack, 64, 1)[:, :64].astype(jnp.bfloat16)
        else:
            out_ref[base:base + BLK, :] = jnp.maximum(left, 0.0).astype(jnp.bfloat16)
            out_ref[base + BLK:base + PACK, :] = jnp.maximum(pack, 0.0).astype(jnp.bfloat16)


def per_device(
    feats, tile_vals, tile_dst, tile_src, tile_count, send_blocks, send_count, w_self, w_nbr, bias
):
    node_rows, cols = feats.shape
    blk_dev = node_rows // BLK
    packed_rows = blk_dev * PACK
    slot_rows = HEAD + packed_rows
    zero_row = PLACES * slot_rows
    tiles = tile_vals.shape[0]
    entries = tiles + blk_dev
    y = lax.axis_index("feat")
    i32 = jnp.int32

    def cut(w):
        here = lax.dynamic_slice_in_dim(w, y * cols, cols, 2)
        return here.reshape(LAYERS, 4, cols, cols)

    ws, wn = cut(w_self), cut(w_nbr)
    w = jnp.concatenate([wn[..., :128], ws[..., :128], wn[..., 128:], ws[..., 128:]], axis=3)
    w = jnp.concatenate(
        [w[:, :, :128].reshape(LAYERS, 512, 384), w[:, :, 128:].reshape(LAYERS, 256, 384)], axis=1
    )
    bias_here = lax.dynamic_slice_in_dim(bias, y * cols, cols, 1)
    b_all = jnp.concatenate(
        [jnp.zeros((LAYERS, 128)), bias_here[:, :128], jnp.zeros((LAYERS, 64)), bias_here[:, 128:]], axis=1
    ).astype(jnp.float32)[:, None, :]

    f3 = feats.reshape(blk_dev, BLK, cols)
    hidden = jnp.concatenate(
        [f3[..., :128], jnp.concatenate([f3[:, :64, 128:], f3[:, 64:, 128:]], axis=2)], axis=1
    ).reshape(packed_rows, LANES)

    table = jnp.zeros((HEAD, LANES), jnp.bfloat16)
    table = table.at[:PEERS, :SLOTS].set(send_blocks[0].astype(jnp.bfloat16))
    table = table.at[:PEERS, SLOTS].set(send_count[0].astype(jnp.bfloat16))

    ids = jnp.arange(tiles, dtype=i32)
    live = ids < tile_count[0]
    dsts = jnp.arange(blk_dev, dtype=i32)
    hits = (tile_dst[None, :] == dsts[:, None]) & live[None, :]
    pairs = (jnp.sum(hits.astype(i32), axis=1) + 1) // 2
    starts = jnp.sum(jnp.where(dsts[None, :] < jnp.arange(blk_dev + 1, dtype=i32)[:, None], pairs[None, :], 0), axis=1)
    before = jnp.sum(jnp.where(dsts[None, :] < tile_dst[:, None], pairs[None, :], 0), axis=1)
    rank = jnp.sum(
        ((tile_dst[None, :] == tile_dst[:, None]) & (ids[None, :] < ids[:, None])).astype(i32), axis=1
    )
    place = jnp.where(live, 2 * before + rank, -1)
    here = place[None, :] == jnp.arange(entries, dtype=i32)[:, None]
    tidx = jnp.sum(jnp.where(here, ids[None, :] - tiles, 0), axis=1) + tiles
    sidx = jnp.sum(jnp.where(here, tile_src[None, :] + 1, 0), axis=1) - 1
    steps = jnp.arange(entries // 2, dtype=i32)
    opens = (steps[:, None] == starts[None, :blk_dev]) & (pairs[None, :] > 0)
    keep = 1.0 - jnp.max(opens.astype(jnp.float32), axis=1)
    ends = jnp.where(pairs > 0, starts[1:], 0)

    NC = len(CHUNKS)
    exchange_call = pl.pallas_call(
        exchange,
        out_shape=(
            jax.ShapeDtypeStruct((PLACES, slot_rows, LANES), jnp.bfloat16),
            jax.ShapeDtypeStruct((packed_rows, LANES), jnp.float32),
        ),
        in_specs=[
            pl.BlockSpec(memory_space=pl.ANY),
            pl.BlockSpec(memory_space=pl.ANY),
            pl.BlockSpec(memory_space=pltpu.VMEM),
            pl.BlockSpec(memory_space=pltpu.VMEM),
        ],
        out_specs=(pl.BlockSpec(memory_space=pl.ANY), pl.BlockSpec(memory_space=pltpu.VMEM)),
        scratch_shapes=[
            pltpu.VMEM((4, packed_rows, LANES), jnp.bfloat16),
            pltpu.VMEM((slot_rows, LANES), jnp.bfloat16),
            pltpu.VMEM((max(CHUNKS) * BLK, 768), jnp.bfloat16),
            pltpu.SemaphoreType.DMA((NC,)),
            pltpu.SemaphoreType.DMA((NC,)),
            pltpu.SemaphoreType.DMA,
            pltpu.SemaphoreType.DMA((4, NC)),
            pltpu.SemaphoreType.DMA((4, NC)),
            pltpu.SemaphoreType.DMA((4, NC)),
            pltpu.SemaphoreType.DMA((4, NC)),
            pltpu.SemaphoreType.DMA((4, NC)),
            pltpu.SemaphoreType.DMA((4, NC)),
        ],
        compiler_params=pltpu.CompilerParams(
            collective_id=0, has_side_effects=True, vmem_limit_bytes=VMEM_BYTES
        ),
        name="exchange",
    )

    def aggregate_call(last):
        out = (node_rows, cols) if last else (packed_rows, LANES)
        return pl.pallas_call(
            functools.partial(aggregate, last),
            out_shape=jax.ShapeDtypeStruct(out, jnp.bfloat16),
            grid_spec=pltpu.PrefetchScalarGridSpec(
                num_scalar_prefetch=4,
                grid=(),
                in_specs=[
                    pl.BlockSpec(memory_space=pl.ANY),
                    pl.BlockSpec(memory_space=pl.ANY),
                    pl.BlockSpec(memory_space=pltpu.VMEM),
                ],
                out_specs=pl.BlockSpec(memory_space=pltpu.VMEM),
                scratch_shapes=[
                    pltpu.VMEM((zero_row + PACK, LANES), jnp.bfloat16),
                    pltpu.VMEM((tiles + 1, BLK, BLK), jnp.bfloat16),
                    pltpu.VMEM((entries // 2 + 1, BLK, 2 * LANES), jnp.float32),
                    pltpu.SemaphoreType.DMA((PLACES,)),
                    pltpu.SemaphoreType.DMA((4,)),
                ],
            ),
            compiler_params=pltpu.CompilerParams(vmem_limit_bytes=VMEM_BYTES),
            name="aggregate_last" if last else "aggregate",
        )

    roff = None
    for layer in range(LAYERS):
        g, s = exchange_call(hidden, table, w[layer], b_all[layer])
        if layer == 0:
            spots = [4 - offset(d) for d in range(PEERS)]
            pick = (jnp.arange(PLACES)[:, None] == jnp.array(spots)[None, :]).astype(jnp.float32)
            heads = jnp.sum(g[:, :PEERS, :16].astype(jnp.float32) * pick[:, :, None], axis=0).astype(i32)
            filled = jnp.arange(SLOTS, dtype=i32)[None, :] < heads[:, SLOTS:SLOTS + 1]
            spot_rows = jnp.array(spots, i32)[:, None] * slot_rows + HEAD
            theirs = jnp.where(filled, spot_rows + PACK * heads[:, :SLOTS], zero_row).reshape(-1)
            mine = 4 * slot_rows + HEAD + PACK * dsts
            rows = jnp.concatenate([mine, theirs])
            srcs = jnp.arange(rows.shape[0], dtype=i32)
            roff = jnp.sum(jnp.where(sidx[:, None] == srcs[None, :], rows[None, :] - zero_row, 0), axis=1) + zero_row
        hidden = aggregate_call(layer == LAYERS - 1)(tidx, roff, keep, ends, g, tile_vals, s)
    return hidden


def solution(mesh):
    in_specs = (
        P("dom", "feat"),
        P("dom", None, None),
        P("dom"),
        P("dom"),
        P("dom"),
        P("dom", None, None),
        P("dom", None),
        P(),
        P(),
        P(),
    )
    out_specs = P("dom", "feat")
    return jax.shard_map(
        per_device, mesh=mesh, in_specs=in_specs, out_specs=out_specs, check_vma=False
    )
```

```python
import functools

import jax
import jax.numpy as jnp
from jax import lax
from jax.experimental import pallas as pl
from jax.experimental.pallas import tpu as pltpu
from jax.sharding import PartitionSpec as P

LAYERS = 3
BLK = 128
PEERS = 8
SLOTS = 8
MESH = pl.DeviceIdType.MESH
LANES = 128
PACK = 192
HEAD = 16
CHUNKS = (4, 4, 4, 4)
AHEAD = 1
PLACES = 9
UNROLL = 8
EXCHANGE_BYTES = 32 * 1024 * 1024
AGGREGATE_BYTES = 40 * 1024 * 1024


def offset(d):
    return (d // 2 + 1) * (1 if d % 2 == 0 else -1)


def cut(raw, odd):
    t0, t1 = raw[:, :128], raw[:, 128:]
    first = jnp.where(odd, jnp.concatenate([t0[:, 64:], t1[:, :64]], axis=1), t0)
    rest = jnp.where(odd, t1[:, 64:], t1[:, :64])
    return first, rest


def order_tiles(count, dst, src, g_ref, idx_ref):
    f32 = jnp.float32
    wide = 2 * LANES
    slot_rows = g_ref.shape[1]
    zero_row = PLACES * slot_rows
    tiles = dst.shape[1]
    pad = jnp.zeros((1, wide - tiles), f32)
    lane = lax.broadcasted_iota(jnp.int32, (1, wide), 1)
    live = lane < count
    dst = jnp.where(live, jnp.concatenate([dst.astype(f32), pad], axis=1), float(wide))
    src = jnp.concatenate([src.astype(f32), pad], axis=1)
    square = (wide, wide)
    row_id = lax.broadcasted_iota(jnp.int32, square, 0).astype(f32)
    col_id = lax.broadcasted_iota(jnp.int32, square, 1).astype(f32)
    dst_row = jnp.broadcast_to(dst, square)
    dst_col = jnp.transpose(dst_row)
    src_col = jnp.transpose(jnp.broadcast_to(src, square))
    rank = jnp.sum(jnp.where((dst_row == dst_col) & (row_id < col_id), 1.0, 0.0), axis=0, keepdims=True)
    many_col = jnp.sum(jnp.where(dst_row == row_id, 1.0, 0.0)[:16], axis=1, keepdims=True)
    many_row = jnp.sum(jnp.where(dst_col == col_id, 1.0, 0.0), axis=0, keepdims=True)
    pairs_col = jnp.floor((many_col + 1.0) * 0.5)
    pairs_row = jnp.where(lane < 16, jnp.floor((many_row + 1.0) * 0.5), 0.0)
    few_row, few_col = row_id[:16], col_id[:16]
    start_col = jnp.sum(jnp.where(few_col < few_row, pairs_row, 0.0), axis=1, keepdims=True)
    before = jnp.sum(jnp.where(few_row < dst, pairs_col, 0.0), axis=0, keepdims=True)
    place = jnp.where(live, 2.0 * before + rank, -1.0)
    hit = jnp.where(jnp.transpose(jnp.broadcast_to(place, square)) == col_id, 1.0, 0.0)
    offs = jnp.where(lane < 16, 4.0 * slot_rows + HEAD + PACK * lane.astype(f32), 0.0)[:, :LANES]
    short = lane[:, :LANES]
    for d in range(PEERS):
        spot = 4 - offset(d)
        table = g_ref[spot, :HEAD, :].astype(f32)[d:d + 1]
        first = jnp.where(short.astype(f32) < table[:, SLOTS:SLOTS + 1], float(spot * slot_rows + HEAD) + PACK * table,
                          float(zero_row))
        first = jnp.where(short < SLOTS, first, 0.0)
        offs = offs + pltpu.roll(jnp.broadcast_to(first, (8, LANES)), 16 + SLOTS * d, 1)[:1]
    offs = jnp.concatenate([offs, jnp.zeros((1, LANES), f32)], axis=1)
    from_col = jnp.sum(jnp.where(src_col == col_id, offs, 0.0), axis=1, keepdims=True)
    opens = jnp.sum(jnp.where((start_col == few_col) & (pairs_col > 0.0), 1.0, 0.0), axis=0, keepdims=True)
    ends = jnp.sum(jnp.where(few_row <= few_col, pairs_col, 0.0), axis=0, keepdims=True)
    rows = (
        jnp.sum(hit * row_id, axis=0, keepdims=True),
        jnp.sum(hit * (from_col - zero_row), axis=0, keepdims=True) + zero_row,
        jnp.sum(hit, axis=0, keepdims=True),
        1.0 - opens,
        jnp.where(pairs_row > 0.0, ends, 0.0),
    )
    for k, row in enumerate(rows):
        idx_ref[k:k + 1, :] = row.astype(jnp.int32)


def exchange(layer, count_ref, h_ref, tab_ref, ws_ref, wn_ref, b_ref, dst_ref, src_ref, g_ref, s_ref, idx_ref,
             held, lhs, raw, w_ref, load_sem, tab_sem, raw_sem, ysend, yrecv, xsend, xrecv, psend, precv):
    i = lax.axis_index("dom")
    y = lax.axis_index("feat")
    n_dom = lax.axis_size("dom")
    core = lax.rem(i, 2)
    y_up, y_down = lax.rem(y + 1, 4), lax.rem(y + 3, 4)
    x_up, x_down = lax.rem(i + 2, n_dom), lax.rem(i + n_dom - 2, n_dom)
    partner = i + 1 - 2 * core
    NC = len(CHUNKS)
    first_row = [sum(CHUNKS[:n]) * PACK for n in range(NC)]

    def hrows(n, part=None):
        size = CHUNKS[n] * PACK
        if part is None:
            return pl.ds(first_row[n], size)
        return pl.ds(first_row[n] + part * (size // 2), size // 2)

    def grows(n):
        size = CHUNKS[n] * PACK
        return pl.ds(0, HEAD + size) if n == 0 else pl.ds(HEAD + first_row[n], size)

    def remote(src, dst, send, recv, dom, feat):
        return pltpu.make_async_remote_copy(
            src_ref=src, dst_ref=dst, send_sem=send, recv_sem=recv,
            device_id=(dom, feat), device_id_type=MESH)

    loads = [pltpu.make_async_copy(h_ref.at[hrows(n)], held.at[y, hrows(n)], load_sem.at[n]) for n in range(NC)]
    for load in loads:
        load.start()
    tab_load = pltpu.make_async_copy(tab_ref, g_ref.at[4, pl.ds(0, HEAD)], tab_sem)
    tab_load.start()
    window = pl.ds(pl.multiple_of((3 * y // 2) * LANES, LANES), 2 * LANES)
    raws = [pltpu.make_async_copy(ref.at[layer, :, window], raw.at[k], raw_sem.at[k]) for k, ref in enumerate((wn_ref, ws_ref))]
    for load in raws:
        load.start()

    barrier = pltpu.get_barrier_semaphore()
    for dom, feat in ((i, y_up), (i, y_down), (x_up, y), (x_down, y), (partner, y)):
        pl.semaphore_signal(barrier, inc=1, device_id=(dom, feat), device_id_type=MESH)
    pl.semaphore_wait(barrier, 5)

    sent = []
    up, down = [], []

    def gather_own(n):
        loads[n].wait()
        a = remote(held.at[y, hrows(n)], held.at[y, hrows(n)], ysend.at[0, n], yrecv.at[0, n], i, y_up)
        b = remote(held.at[y, hrows(n)], held.at[y, hrows(n)], ysend.at[1, n], yrecv.at[1, n], i, y_down)
        a.start()
        b.start()
        up.append(a)
        down.append(b)
        sent.extend([a, b])

    for n in range(min(AHEAD, NC)):
        gather_own(n)

    def gather_relay(n):
        up[n].wait_recv()
        a = remote(held.at[y_down, hrows(n, 0)], held.at[y_down, hrows(n, 0)], ysend.at[2, n], yrecv.at[2, n], i, y_up)
        a.start()
        down[n].wait_recv()
        b = remote(held.at[y_up, hrows(n, 1)], held.at[y_up, hrows(n, 1)], ysend.at[3, n], yrecv.at[3, n], i, y_down)
        b.start()
        sent.extend([a, b])
        if n + AHEAD < NC:
            gather_own(n + AHEAD)
        return a, b

    lane = lax.broadcasted_iota(jnp.int32, (64, LANES), 1)
    low = lane < 64

    def project(n):
        blocks = CHUNKS[n]
        for j in range(blocks):
            base = first_row[n] + j * PACK
            out = slice(j * BLK, (j + 1) * BLK)
            top = slice(j * BLK, j * BLK + 64)
            bot = slice(j * BLK + 64, (j + 1) * BLK)
            for a in range(4):
                lhs[out, a * LANES:(a + 1) * LANES] = held[a, base:base + BLK, :]
            for pair in range(2):
                p0 = held[2 * pair, base + BLK:base + PACK, :]
                p1 = held[2 * pair + 1, base + BLK:base + PACK, :]
                cols = slice(512 + pair * LANES, 512 + (pair + 1) * LANES)
                lhs[top, cols] = jnp.concatenate([p0[:, :64], p1[:, :64]], axis=1)
                lhs[bot, cols] = jnp.concatenate([p0[:, 64:], p1[:, 64:]], axis=1)
        res = jnp.dot(lhs[:blocks * BLK], w_ref[...], preferred_element_type=jnp.float32) + bias
        for j in range(blocks):
            r0 = j * BLK
            base = first_row[n] + j * PACK
            g_ref[4, HEAD + base:HEAD + base + BLK, :] = res[r0:r0 + BLK, :LANES].astype(jnp.bfloat16)
            s_ref[base:base + BLK, :] = res[r0:r0 + BLK, LANES:2 * LANES]
            top = res[r0:r0 + 64, 2 * LANES:]
            bot = res[r0 + 64:r0 + BLK, 2 * LANES:]
            g_ref[4, HEAD + base + BLK:HEAD + base + PACK, :] = jnp.where(
                low, top, pltpu.roll(bot, 64, 1)).astype(jnp.bfloat16)
            s_ref[base + BLK:base + PACK, :] = jnp.where(low, pltpu.roll(top, 64, 1), bot)

    ours, first, second = [], [], []

    def send_own(n):
        src = g_ref.at[4, grows(n)]
        a = remote(src, g_ref.at[2, grows(n)], xsend.at[0, n], xrecv.at[0, n], x_up, y)
        b = remote(src, g_ref.at[6, grows(n)], xsend.at[1, n], xrecv.at[1, n], x_down, y)
        c = remote(src, g_ref.at[3 + 2 * core, grows(n)], psend.at[0, n], precv.at[0, n], partner, y)
        for copy in (a, b, c):
            copy.start()
        ours.append((a, b, c))
        sent.extend([a, b, c])

    def relay_one(n):
        a, b, _ = ours[n]
        a.wait_recv()
        u = remote(g_ref.at[2, grows(n)], g_ref.at[0, grows(n)], xsend.at[2, n], xrecv.at[2, n], x_up, y)
        pu = remote(g_ref.at[2, grows(n)], g_ref.at[1 + 2 * core, grows(n)], psend.at[1, n], precv.at[1, n], partner, y)
        u.start()
        pu.start()
        b.wait_recv()
        v = remote(g_ref.at[6, grows(n)], g_ref.at[8, grows(n)], xsend.at[3, n], xrecv.at[3, n], x_down, y)
        pv = remote(g_ref.at[6, grows(n)], g_ref.at[5 + 2 * core, grows(n)], psend.at[2, n], precv.at[2, n], partner, y)
        v.start()
        pv.start()
        first.append((u, v, pu, pv))
        sent.extend([u, v, pu, pv])

    def relay_two(n):
        u, v, _, _ = first[n]
        u.wait_recv()
        v.wait_recv()
        c = remote(g_ref.at[8 - 8 * core, grows(n)], g_ref.at[7 - 6 * core, grows(n)], psend.at[3, n], precv.at[3, n],
                   partner, y)
        c.start()
        second.append(c)
        sent.append(c)

    g_ref[PLACES, :PACK, :] = jnp.zeros((PACK, LANES), jnp.bfloat16)
    odd = lax.rem(y, 2) == 1
    for load in raws:
        load.wait()
    n_first, n_rest = cut(raw[0], odd)
    s_first, s_rest = cut(raw[1], odd)
    rest = jnp.concatenate([n_rest, s_rest], axis=1)
    for a in range(4):
        for part, cols in ((n_first, 0), (s_first, 1), (rest, 2)):
            cols = slice(cols * LANES, (cols + 1) * LANES)
            w_ref[a * BLK:(a + 1) * BLK, cols] = part[a * PACK:a * PACK + BLK]
            w_ref[512 + a * 64:512 + (a + 1) * 64, cols] = part[a * PACK + BLK:(a + 1) * PACK]
    b_first, b_rest = cut(b_ref[layer:layer + 1, window], odd)
    bias = jnp.concatenate([jnp.zeros((1, LANES), jnp.float32), b_first, jnp.zeros((1, 64), jnp.float32), b_rest], axis=1)

    tab_load.wait()
    for n in range(NC):
        a, b = gather_relay(n)
        a.wait_recv()
        b.wait_recv()
        project(n)
        send_own(n)
        if n >= 1:
            relay_one(n - 1)
        if n >= 2:
            relay_two(n - 2)
    relay_one(NC - 1)
    for n in range(1):
        ours[n][2].wait_recv()
        first[n][2].wait_recv()
        first[n][3].wait_recv()
        second[n].wait_recv()
    order_tiles(count_ref[0], dst_ref[...], src_ref[...], g_ref, idx_ref)
    for n in range(max(NC - 2, 0), NC):
        relay_two(n)
    for n in range(1, NC):
        ours[n][2].wait_recv()
        first[n][2].wait_recv()
        first[n][3].wait_recv()
        second[n].wait_recv()
    for copy in sent:
        copy.wait_send()


def aggregate(last, idx, gv, tv, s_ref, out_ref, part):
    lane = lax.broadcasted_iota(jnp.int32, (64, LANES), 1)
    low = lane < 64

    def source(q):
        row = pl.multiple_of(idx[1, q], 16)
        ones = jnp.full((64, 64), idx[2, q].astype(jnp.float32)).astype(jnp.bfloat16)
        left = gv[pl.ds(row, BLK), :]
        pack = gv[pl.ds(row + BLK, 64), :]
        right = jnp.concatenate([
            jnp.concatenate([pack[:, :64], ones], axis=1),
            jnp.concatenate([pack[:, 64:], ones], axis=1),
        ], axis=0)
        return jnp.concatenate([left, right], axis=1)

    def product(p):
        q = 2 * p
        lhs = jnp.concatenate([tv[idx[0, q]], tv[idx[0, q + 1]]], axis=1)
        rhs = jnp.concatenate([source(q), source(q + 1)], axis=0)
        return jnp.dot(lhs, rhs, preferred_element_type=jnp.float32)

    part[0] = jnp.zeros(part.shape[1:], jnp.float32)

    def step(g, carry):
        products = [product(g * UNROLL + u) for u in range(UNROLL)]
        for u in range(UNROLL):
            p = g * UNROLL + u
            part[p + 1] = part[p] * idx[3, p].astype(jnp.float32) + products[u]
        return carry

    lax.fori_loop(0, (part.shape[0] - 1) // UNROLL, step, 0)

    for b in range(s_ref.shape[0] // PACK):
        acc = part[idx[4, b]]
        scale = 1.0 / (1.0 + acc[:, PACK:PACK + 1])
        left = acc[:, :LANES] * scale
        right = acc[:, LANES:] * scale
        pack = jnp.where(low, right[:64], pltpu.roll(right[64:], 64, 1))
        base = b * PACK
        left = left + s_ref[base:base + BLK, :]
        pack = pack + s_ref[base + BLK:base + PACK, :]
        if last:
            row = b * BLK
            out_ref[row:row + BLK, :LANES] = left.astype(jnp.bfloat16)
            out_ref[row:row + 64, LANES:] = pack[:, :64].astype(jnp.bfloat16)
            out_ref[row + 64:row + BLK, LANES:] = pltpu.roll(pack, 64, 1)[:, :64].astype(jnp.bfloat16)
        else:
            out_ref[base:base + BLK, :] = jnp.maximum(left, 0.0).astype(jnp.bfloat16)
            out_ref[base + BLK:base + PACK, :] = jnp.maximum(pack, 0.0).astype(jnp.bfloat16)


def per_device(
    feats, tile_vals, tile_dst, tile_src, tile_count, send_blocks, send_count, w_self, w_nbr, bias
):
    node_rows, cols = feats.shape
    blk_dev = node_rows // BLK
    packed_rows = blk_dev * PACK
    slot_rows = HEAD + packed_rows
    tiles = tile_vals.shape[0]
    entries = tiles + blk_dev

    f3 = feats.reshape(blk_dev, BLK, cols)
    hidden = jnp.concatenate(
        [f3[..., :128], jnp.concatenate([f3[:, :64, 128:], f3[:, 64:, 128:]], axis=2)], axis=1
    ).reshape(packed_rows, LANES)

    table = jnp.concatenate([send_blocks[0], send_count[0][:, None]], axis=1).astype(jnp.bfloat16)
    table = jnp.pad(table, ((0, HEAD - PEERS), (0, LANES - SLOTS - 1)))

    NC = len(CHUNKS)
    vmem = pl.BlockSpec(memory_space=pltpu.VMEM)
    hbm = pl.BlockSpec(memory_space=pl.ANY)

    def exchange_call(layer):
        return pl.pallas_call(
            functools.partial(exchange, layer),
            out_shape=(
                jax.ShapeDtypeStruct((PLACES + 1, slot_rows, LANES), jnp.bfloat16),
                jax.ShapeDtypeStruct((packed_rows, LANES), jnp.float32),
                jax.ShapeDtypeStruct((8, 2 * LANES), jnp.int32),
            ),
            in_specs=[pl.BlockSpec(memory_space=pltpu.SMEM), hbm, hbm, hbm, hbm, vmem, vmem, vmem],
            out_specs=(vmem, vmem, vmem),
            scratch_shapes=[
                pltpu.VMEM((4, packed_rows, LANES), jnp.bfloat16),
                pltpu.VMEM((max(CHUNKS) * BLK, 768), jnp.bfloat16),
                pltpu.VMEM((2, 768, 2 * LANES), jnp.bfloat16),
                pltpu.VMEM((768, 3 * LANES), jnp.bfloat16),
                pltpu.SemaphoreType.DMA((NC,)),
                pltpu.SemaphoreType.DMA,
                pltpu.SemaphoreType.DMA((2,)),
            ] + [pltpu.SemaphoreType.DMA((4, NC)) for _ in range(6)],
            compiler_params=pltpu.CompilerParams(
                collective_id=layer, has_side_effects=True, vmem_limit_bytes=EXCHANGE_BYTES
            ),
            name=f"exchange{layer}",
        )

    def aggregate_call(last):
        out = (node_rows, cols) if last else (packed_rows, LANES)
        return pl.pallas_call(
            functools.partial(aggregate, last),
            out_shape=jax.ShapeDtypeStruct(out, jnp.bfloat16),
            grid_spec=pltpu.PrefetchScalarGridSpec(
                num_scalar_prefetch=1,
                grid=(),
                in_specs=[vmem, vmem, vmem],
                out_specs=vmem,
                scratch_shapes=[pltpu.VMEM((entries // 2 + 1, BLK, 2 * LANES), jnp.float32)],
            ),
            compiler_params=pltpu.CompilerParams(vmem_limit_bytes=AGGREGATE_BYTES),
            name="aggregate_last" if last else "aggregate",
        )

    dsts, srcs = tile_dst[None, :], tile_src[None, :]
    for layer in range(LAYERS):
        g, s, idx = exchange_call(layer)(tile_count, hidden, table, w_self, w_nbr, bias, dsts, srcs)
        g = g.reshape((PLACES + 1) * slot_rows, LANES)
        hidden = aggregate_call(layer == LAYERS - 1)(idx, g, tile_vals, s)
    return hidden


def solution(mesh):
    in_specs = (
        P("dom", "feat"),
        P("dom", None, None),
        P("dom"),
        P("dom"),
        P("dom"),
        P("dom", None, None),
        P("dom", None),
        P(),
        P(),
        P(),
    )
    out_specs = P("dom", "feat")
    return jax.shard_map(
        per_device, mesh=mesh, in_specs=in_specs, out_specs=out_specs, check_vma=False
    )
```

```python
import functools

import jax
import jax.numpy as jnp
from jax import lax
from jax.experimental import pallas as pl
from jax.experimental.pallas import tpu as pltpu
from jax.sharding import PartitionSpec as P

LAYERS = 3
BLK = 128
PEERS = 8
SLOTS = 8
MESH = pl.DeviceIdType.MESH
LANES = 128
PACK = 192
HEAD = 16
CHUNKS = (4, 4, 4, 4)
GROUPS = 4
AHEAD = 2
PLACES = 9
UNROLL = 8
EXCHANGE_BYTES = 14 * 1024 * 1024
AGGREGATE_BYTES = 17 * 1024 * 1024


def offset(d):
    return (d // 2 + 1) * (1 if d % 2 == 0 else -1)


def cut(raw, odd):
    t0, t1 = raw[:, :128], raw[:, 128:]
    first = jnp.where(odd, jnp.concatenate([t0[:, 64:], t1[:, :64]], axis=1), t0)
    rest = jnp.where(odd, t1[:, 64:], t1[:, :64])
    return first, rest


def order_tiles(count, dst, src, core, g_ref, idx_ref):
    f32 = jnp.float32
    wide = 2 * LANES
    slot_rows = g_ref.shape[1]
    zero_row = PLACES * slot_rows
    tiles = dst.shape[1]
    pad = jnp.zeros((1, wide - tiles), f32)
    lane = lax.broadcasted_iota(jnp.int32, (1, wide), 1)
    live = lane < count
    dst = jnp.where(live, jnp.concatenate([dst.astype(f32), pad], axis=1), float(wide))
    src = jnp.concatenate([src.astype(f32), pad], axis=1)
    square = (wide, wide)
    row_id = lax.broadcasted_iota(jnp.int32, square, 0).astype(f32)
    col_id = lax.broadcasted_iota(jnp.int32, square, 1).astype(f32)
    dst_row = jnp.broadcast_to(dst, square)
    dst_col = jnp.transpose(dst_row)
    src_col = jnp.transpose(jnp.broadcast_to(src, square))
    rank = jnp.sum(jnp.where((dst_row == dst_col) & (row_id < col_id), 1.0, 0.0), axis=0, keepdims=True)
    many_col = jnp.sum(jnp.where(dst_row == row_id, 1.0, 0.0)[:16], axis=1, keepdims=True)
    many_row = jnp.sum(jnp.where(dst_col == col_id, 1.0, 0.0), axis=0, keepdims=True)
    pairs_col = jnp.floor((many_col + 1.0) * 0.5)
    pairs_row = jnp.where(lane < 16, jnp.floor((many_row + 1.0) * 0.5), 0.0)
    few_row, few_col = row_id[:16], col_id[:16]
    start_col = jnp.sum(jnp.where(few_col < few_row, pairs_row, 0.0), axis=1, keepdims=True)
    before = jnp.sum(jnp.where(few_row < dst, pairs_col, 0.0), axis=0, keepdims=True)
    place = jnp.where(live, 2.0 * before + rank, -1.0)
    hit = jnp.where(jnp.transpose(jnp.broadcast_to(place, square)) == col_id, 1.0, 0.0)
    offs = jnp.where(lane < 16, 4.0 * slot_rows + HEAD + PACK * lane.astype(f32), 0.0)[:, :LANES]
    short = lane[:, :LANES]
    for d in range(PEERS):
        spot = 4 - offset(d)
        table = g_ref[spot, :HEAD, :].astype(f32)[d:d + 1]
        block = table
        if spot in (0, 8):
            block = jnp.where(core == spot // 8, short.astype(f32), table)
        first = jnp.where(short.astype(f32) < table[:, SLOTS:SLOTS + 1], float(spot * slot_rows + HEAD) + PACK * block,
                          float(zero_row))
        first = jnp.where(short < SLOTS, first, 0.0)
        offs = offs + pltpu.roll(jnp.broadcast_to(first, (8, LANES)), 16 + SLOTS * d, 1)[:1]
    offs = jnp.concatenate([offs, jnp.zeros((1, LANES), f32)], axis=1)
    from_col = jnp.sum(jnp.where(src_col == col_id, offs, 0.0), axis=1, keepdims=True)
    opens = jnp.sum(jnp.where((start_col == few_col) & (pairs_col > 0.0), 1.0, 0.0), axis=0, keepdims=True)
    ends = jnp.sum(jnp.where(few_row <= few_col, pairs_col, 0.0), axis=0, keepdims=True)
    rows = (
        jnp.sum(hit * row_id, axis=0, keepdims=True),
        jnp.sum(hit * (from_col - zero_row), axis=0, keepdims=True) + zero_row,
        jnp.sum(hit, axis=0, keepdims=True),
        1.0 - opens,
        jnp.where(pairs_row > 0.0, ends, 0.0),
    )
    for k, row in enumerate(rows):
        idx_ref[k:k + 1, :] = row.astype(jnp.int32)


def exchange(layer, count_ref, h_ref, tab_ref, ws_ref, wn_ref, b_ref, dst_ref, src_ref, g_ref, s_ref, idx_ref,
             held, lhs, raw, w_ref, picked, load_sem, tab_sem, raw_sem, ysend, yrecv, xsend, xrecv, psend, precv):
    i = lax.axis_index("dom")
    y = lax.axis_index("feat")
    n_dom = lax.axis_size("dom")
    core = lax.rem(i, 2)
    y_up, y_down = lax.rem(y + 1, 4), lax.rem(y + 3, 4)
    x_up, x_down = lax.rem(i + 2, n_dom), lax.rem(i + n_dom - 2, n_dom)
    partner = i + 1 - 2 * core
    NC = len(CHUNKS)
    first_row = [sum(CHUNKS[:n]) * PACK for n in range(NC)]

    def hrows(n, part=None):
        size = CHUNKS[n] * PACK
        if part is None:
            return pl.ds(first_row[n], size)
        return pl.ds(first_row[n] + part * (size // 2), size // 2)

    def grows(n):
        size = CHUNKS[n] * PACK
        return pl.ds(0, HEAD + size) if n == 0 else pl.ds(HEAD + first_row[n], size)

    def remote(src, dst, send, recv, dom, feat):
        return pltpu.make_async_remote_copy(
            src_ref=src, dst_ref=dst, send_sem=send, recv_sem=recv,
            device_id=(dom, feat), device_id_type=MESH)

    loads = [pltpu.make_async_copy(h_ref.at[hrows(n)], held.at[y, hrows(n)], load_sem.at[n]) for n in range(NC)]
    for load in loads:
        load.start()
    tab_load = pltpu.make_async_copy(tab_ref, g_ref.at[4, pl.ds(0, HEAD)], tab_sem)
    tab_load.start()
    window = pl.ds(pl.multiple_of((3 * y // 2) * LANES, LANES), 2 * LANES)
    raws = [pltpu.make_async_copy(ref.at[layer, :, window], raw.at[k], raw_sem.at[k]) for k, ref in enumerate((wn_ref, ws_ref))]
    for load in raws:
        load.start()

    barrier = pltpu.get_barrier_semaphore()
    for dom, feat in ((i, y_up), (i, y_down), (x_up, y), (x_down, y), (partner, y)):
        pl.semaphore_signal(barrier, inc=1, device_id=(dom, feat), device_id_type=MESH)
    pl.semaphore_wait(barrier, 5)

    sent = []
    up, down = [], []

    def gather_own(n):
        loads[n].wait()
        a = remote(held.at[y, hrows(n)], held.at[y, hrows(n)], ysend.at[0, n], yrecv.at[0, n], i, y_up)
        b = remote(held.at[y, hrows(n)], held.at[y, hrows(n)], ysend.at[1, n], yrecv.at[1, n], i, y_down)
        a.start()
        b.start()
        up.append(a)
        down.append(b)
        sent.extend([a, b])

    for n in range(min(AHEAD, NC)):
        gather_own(n)

    def gather_relay(n):
        up[n].wait_recv()
        a = remote(held.at[y_down, hrows(n, 0)], held.at[y_down, hrows(n, 0)], ysend.at[2, n], yrecv.at[2, n], i, y_up)
        a.start()
        down[n].wait_recv()
        b = remote(held.at[y_up, hrows(n, 1)], held.at[y_up, hrows(n, 1)], ysend.at[3, n], yrecv.at[3, n], i, y_down)
        b.start()
        sent.extend([a, b])
        if n + AHEAD < NC:
            gather_own(n + AHEAD)
        return a, b

    lane = lax.broadcasted_iota(jnp.int32, (64, LANES), 1)
    low = lane < 64

    def project(n):
        blocks = CHUNKS[n]
        for j in range(blocks):
            base = first_row[n] + j * PACK
            out = slice(j * BLK, (j + 1) * BLK)
            top = slice(j * BLK, j * BLK + 64)
            bot = slice(j * BLK + 64, (j + 1) * BLK)
            for a in range(4):
                lhs[out, a * LANES:(a + 1) * LANES] = held[a, base:base + BLK, :]
            for pair in range(2):
                p0 = held[2 * pair, base + BLK:base + PACK, :]
                p1 = held[2 * pair + 1, base + BLK:base + PACK, :]
                cols = slice(512 + pair * LANES, 512 + (pair + 1) * LANES)
                lhs[top, cols] = jnp.concatenate([p0[:, :64], p1[:, :64]], axis=1)
                lhs[bot, cols] = jnp.concatenate([p0[:, 64:], p1[:, 64:]], axis=1)
        res = jnp.dot(lhs[:blocks * BLK], w_ref[...], preferred_element_type=jnp.float32) + bias
        for j in range(blocks):
            r0 = j * BLK
            base = first_row[n] + j * PACK
            g_ref[4, HEAD + base:HEAD + base + BLK, :] = res[r0:r0 + BLK, :LANES].astype(jnp.bfloat16)
            s_ref[base:base + BLK, :] = res[r0:r0 + BLK, LANES:2 * LANES]
            top = res[r0:r0 + 64, 2 * LANES:]
            bot = res[r0 + 64:r0 + BLK, 2 * LANES:]
            g_ref[4, HEAD + base + BLK:HEAD + base + PACK, :] = jnp.where(
                low, top, pltpu.roll(bot, 64, 1)).astype(jnp.bfloat16)
            s_ref[base + BLK:base + PACK, :] = jnp.where(low, pltpu.roll(top, 64, 1), bot)

    whole_to = x_down + core * (x_up - x_down)
    whole_from, whole_at = 6 - 4 * core, 8 - 8 * core
    list_to = x_up + core * (x_down - x_up)
    list_from, list_at = 2 + 4 * core, 8 * core
    ours, first, second, listed = [], [], [], []

    def group(m):
        size = sum(CHUNKS) // GROUPS * PACK
        return pl.ds(0, HEAD + size) if m == 0 else pl.ds(HEAD + m * size, size)

    def send_own(n):
        src = g_ref.at[4, grows(n)]
        a = remote(src, g_ref.at[2, grows(n)], xsend.at[0, n], xrecv.at[0, n], x_up, y)
        b = remote(src, g_ref.at[6, grows(n)], xsend.at[1, n], xrecv.at[1, n], x_down, y)
        c = remote(src, g_ref.at[3 + 2 * core, grows(n)], psend.at[0, n], precv.at[0, n], partner, y)
        for copy in (a, b, c):
            copy.start()
        ours.append((a, b, c))
        sent.extend([a, b, c])

    def relay_group(m):
        per = NC // GROUPS
        for n in range(m * per, (m + 1) * per):
            ours[n][0].wait_recv()
            ours[n][1].wait_recv()
        u = remote(g_ref.at[whole_from, group(m)], g_ref.at[whole_at, group(m)], xsend.at[2, m], xrecv.at[2, m], whole_to, y)
        pu = remote(g_ref.at[2, group(m)], g_ref.at[1 + 2 * core, group(m)], psend.at[1, m], precv.at[1, m], partner, y)
        pv = remote(g_ref.at[6, group(m)], g_ref.at[5 + 2 * core, group(m)], psend.at[2, m], precv.at[2, m], partner, y)
        for copy in (u, pu, pv):
            copy.start()
        first.append((u, pu, pv))
        sent.extend([u, pu, pv])

    def relay_list():
        picked[:HEAD, :] = g_ref[list_from, :HEAD, :]
        table = g_ref[list_from, :HEAD, :].astype(jnp.float32)
        wanted = jnp.where(core == 1, table[7:8], table[6:7])
        short = lax.broadcasted_iota(jnp.int32, (1, LANES), 1)

        def pick(s, carry):
            block = jnp.sum(jnp.where(short == s, wanted, 0.0), axis=1, keepdims=True)
            block = jnp.broadcast_to(block, (16, LANES))
            total = jnp.zeros((PACK // 16, 16, LANES), jnp.bfloat16)
            for j in range(sum(CHUNKS)):
                one = jnp.where(block == float(j), 1.0, 0.0).astype(jnp.bfloat16)
                rows = g_ref[list_from, HEAD + j * PACK:HEAD + (j + 1) * PACK, :]
                total = total + rows.reshape(PACK // 16, 16, LANES) * one[None]
            picked[pl.ds(pl.multiple_of(HEAD + s * PACK, 16), PACK), :] = total.reshape(PACK, LANES)
            return carry

        lax.fori_loop(0, SLOTS, pick, 0)
        copy = remote(picked, g_ref.at[list_at, pl.ds(0, HEAD + SLOTS * PACK)], xsend.at[3, 0], xrecv.at[3, 0], list_to, y)
        copy.start()
        listed.append(copy)
        sent.append(copy)

    def relay_two(m):
        first[m][0].wait_recv()
        c = remote(g_ref.at[whole_at, group(m)], g_ref.at[7 - 6 * core, group(m)], psend.at[3, m], precv.at[3, m], partner, y)
        c.start()
        second.append(c)
        sent.append(c)

    g_ref[PLACES, :PACK, :] = jnp.zeros((PACK, LANES), jnp.bfloat16)
    odd = lax.rem(y, 2) == 1
    for load in raws:
        load.wait()
    n_first, n_rest = cut(raw[0], odd)
    s_first, s_rest = cut(raw[1], odd)
    rest = jnp.concatenate([n_rest, s_rest], axis=1)
    for a in range(4):
        for part, cols in ((n_first, 0), (s_first, 1), (rest, 2)):
            cols = slice(cols * LANES, (cols + 1) * LANES)
            w_ref[a * BLK:(a + 1) * BLK, cols] = part[a * PACK:a * PACK + BLK]
            w_ref[512 + a * 64:512 + (a + 1) * 64, cols] = part[a * PACK + BLK:(a + 1) * PACK]
    b_first, b_rest = cut(b_ref[layer:layer + 1, window], odd)
    bias = jnp.concatenate([jnp.zeros((1, LANES), jnp.float32), b_first, jnp.zeros((1, 64), jnp.float32), b_rest], axis=1)

    tab_load.wait()
    relays = [gather_relay(0)]
    for n in range(NC):
        for relay in relays[n]:
            relay.wait_recv()
        project(n)
        send_own(n)
        if n + 1 < NC:
            relays.append(gather_relay(n + 1))
        for m in range(GROUPS):
            if n == min((m + 1) * (NC // GROUPS), NC - 1):
                relay_group(m)
    relay_list()
    for m in range(GROUPS):
        relay_two(m)
    for n in range(NC):
        ours[n][2].wait_recv()
    for m in range(GROUPS):
        first[m][1].wait_recv()
        first[m][2].wait_recv()
        second[m].wait_recv()
    listed[0].wait_recv()
    if layer == 0:
        order_tiles(count_ref[0], dst_ref[...], src_ref[...], core, g_ref, idx_ref)
    else:
        idx_ref[...] = jnp.zeros(idx_ref.shape, idx_ref.dtype)
    for copy in sent:
        copy.wait_send()


def aggregate(last, idx, gv, tv, s_ref, out_ref, part):
    lane = lax.broadcasted_iota(jnp.int32, (64, LANES), 1)
    low = lane < 64

    def source(q):
        row = pl.multiple_of(idx[1, q], 16)
        ones = jnp.full((64, 64), idx[2, q].astype(jnp.float32)).astype(jnp.bfloat16)
        left = gv[pl.ds(row, BLK), :]
        pack = gv[pl.ds(row + BLK, 64), :]
        right = jnp.concatenate([
            jnp.concatenate([pack[:, :64], ones], axis=1),
            jnp.concatenate([pack[:, 64:], ones], axis=1),
        ], axis=0)
        return jnp.concatenate([left, right], axis=1)

    def product(p):
        q = 2 * p
        lhs = jnp.concatenate([tv[idx[0, q]], tv[idx[0, q + 1]]], axis=1)
        rhs = jnp.concatenate([source(q), source(q + 1)], axis=0)
        return jnp.dot(lhs, rhs, preferred_element_type=jnp.float32)

    part[0] = jnp.zeros(part.shape[1:], jnp.float32)

    def step(g, carry):
        products = [product(g * UNROLL + u) for u in range(UNROLL)]
        for u in range(UNROLL):
            p = g * UNROLL + u
            part[p + 1] = part[p] * idx[3, p].astype(jnp.float32) + products[u]
        return carry

    lax.fori_loop(0, (part.shape[0] - 1) // UNROLL, step, 0)

    for b in range(s_ref.shape[0] // PACK):
        acc = part[idx[4, b]]
        scale = 1.0 / (1.0 + acc[:, PACK:PACK + 1])
        left = acc[:, :LANES] * scale
        right = acc[:, LANES:] * scale
        pack = jnp.where(low, right[:64], pltpu.roll(right[64:], 64, 1))
        base = b * PACK
        left = left + s_ref[base:base + BLK, :]
        pack = pack + s_ref[base + BLK:base + PACK, :]
        if last:
            row = b * BLK
            out_ref[row:row + BLK, :LANES] = left.astype(jnp.bfloat16)
            out_ref[row:row + 64, LANES:] = pack[:, :64].astype(jnp.bfloat16)
            out_ref[row + 64:row + BLK, LANES:] = pltpu.roll(pack, 64, 1)[:, :64].astype(jnp.bfloat16)
        else:
            out_ref[base:base + BLK, :] = jnp.maximum(left, 0.0).astype(jnp.bfloat16)
            out_ref[base + BLK:base + PACK, :] = jnp.maximum(pack, 0.0).astype(jnp.bfloat16)


def per_device(
    feats, tile_vals, tile_dst, tile_src, tile_count, send_blocks, send_count, w_self, w_nbr, bias
):
    node_rows, cols = feats.shape
    blk_dev = node_rows // BLK
    packed_rows = blk_dev * PACK
    slot_rows = HEAD + packed_rows
    tiles = tile_vals.shape[0]
    entries = tiles + blk_dev

    f3 = feats.reshape(blk_dev, BLK, cols)
    hidden = jnp.concatenate(
        [f3[..., :128], jnp.concatenate([f3[:, :64, 128:], f3[:, 64:, 128:]], axis=2)], axis=1
    ).reshape(packed_rows, LANES)

    table = jnp.concatenate([send_blocks[0], send_count[0][:, None]], axis=1).astype(jnp.bfloat16)
    table = jnp.pad(table, ((0, HEAD - PEERS), (0, LANES - SLOTS - 1)))

    NC = len(CHUNKS)
    vmem = pl.BlockSpec(memory_space=pltpu.VMEM)
    anywhere = pl.BlockSpec(memory_space=pl.ANY)
    hbm = pl.BlockSpec(memory_space=pltpu.HBM)

    def exchange_call(layer):
        return pl.pallas_call(
            functools.partial(exchange, layer),
            out_shape=(
                jax.ShapeDtypeStruct((PLACES + 1, slot_rows, LANES), jnp.bfloat16),
                jax.ShapeDtypeStruct((packed_rows, LANES), jnp.float32),
                jax.ShapeDtypeStruct((8, 2 * LANES), jnp.int32),
            ),
            in_specs=[pl.BlockSpec(memory_space=pltpu.SMEM), anywhere, anywhere, hbm, hbm, vmem, vmem, vmem],
            out_specs=(vmem, vmem, vmem),
            scratch_shapes=[
                pltpu.VMEM((4, packed_rows, LANES), jnp.bfloat16),
                pltpu.VMEM((max(CHUNKS) * BLK, 768), jnp.bfloat16),
                pltpu.VMEM((2, 768, 2 * LANES), jnp.bfloat16),
                pltpu.VMEM((768, 3 * LANES), jnp.bfloat16),
                pltpu.VMEM((HEAD + SLOTS * PACK, LANES), jnp.bfloat16),
                pltpu.SemaphoreType.DMA((NC,)),
                pltpu.SemaphoreType.DMA,
                pltpu.SemaphoreType.DMA((2,)),
            ] + [pltpu.SemaphoreType.DMA((4, NC)) for _ in range(6)],
            compiler_params=pltpu.CompilerParams(
                collective_id=layer, has_side_effects=True, vmem_limit_bytes=EXCHANGE_BYTES
            ),
            name=f"exchange{layer}",
        )

    def aggregate_call(last):
        out = (node_rows, cols) if last else (packed_rows, LANES)
        return pl.pallas_call(
            functools.partial(aggregate, last),
            out_shape=jax.ShapeDtypeStruct(out, jnp.bfloat16),
            grid_spec=pltpu.PrefetchScalarGridSpec(
                num_scalar_prefetch=1,
                grid=(),
                in_specs=[vmem, vmem, vmem],
                out_specs=vmem,
                scratch_shapes=[pltpu.VMEM((entries // 2 + 1, BLK, 2 * LANES), jnp.float32)],
            ),
            compiler_params=pltpu.CompilerParams(vmem_limit_bytes=AGGREGATE_BYTES),
            name="aggregate_last" if last else "aggregate",
        )

    dsts, srcs = tile_dst[None, :], tile_src[None, :]
    for layer in range(LAYERS):
        g, s, order = exchange_call(layer)(tile_count, hidden, table, w_self, w_nbr, bias, dsts, srcs)
        idx = order if layer == 0 else idx
        g = g.reshape((PLACES + 1) * slot_rows, LANES)
        hidden = aggregate_call(layer == LAYERS - 1)(idx, g, tile_vals, s)
    return hidden


def solution(mesh):
    in_specs = (
        P("dom", "feat"),
        P("dom", None, None),
        P("dom"),
        P("dom"),
        P("dom"),
        P("dom", None, None),
        P("dom", None),
        P(),
        P(),
        P(),
    )
    out_specs = P("dom", "feat")
    return jax.shard_map(
        per_device, mesh=mesh, in_specs=in_specs, out_specs=out_specs, check_vma=False
    )
```

```python
import functools

import jax
import jax.numpy as jnp
from jax import lax
from jax.experimental import pallas as pl
from jax.experimental.pallas import tpu as pltpu
from jax.sharding import PartitionSpec as P

LAYERS = 3
BLK = 128
PEERS = 8
SLOTS = 8
MESH = pl.DeviceIdType.MESH
LANES = 128
PACK = 192
HEAD = 16
CHUNKS = (4, 4, 4, 4)
GROUPS = 4
AHEAD = 2
PLACES = 9
UNROLL = 26
EXCHANGE_BYTES = 14 * 1024 * 1024
AGGREGATE_BYTES = 17 * 1024 * 1024


def offset(d):
    return (d // 2 + 1) * (1 if d % 2 == 0 else -1)


def cut(raw, odd):
    t0, t1 = raw[:, :128], raw[:, 128:]
    first = jnp.where(odd, jnp.concatenate([t0[:, 64:], t1[:, :64]], axis=1), t0)
    rest = jnp.where(odd, t1[:, 64:], t1[:, :64])
    return first, rest


def order_tiles(count, dst, src, core, g_ref, idx_ref):
    f32 = jnp.float32
    wide = 2 * LANES
    slot_rows = g_ref.shape[1]
    zero_row = PLACES * slot_rows
    tiles = dst.shape[1]
    pad = jnp.zeros((1, wide - tiles), f32)
    lane = lax.broadcasted_iota(jnp.int32, (1, wide), 1)
    live = lane < count
    dst = jnp.where(live, jnp.concatenate([dst.astype(f32), pad], axis=1), float(wide))
    src = jnp.concatenate([src.astype(f32), pad], axis=1)
    square = (wide, wide)
    row_id = lax.broadcasted_iota(jnp.int32, square, 0).astype(f32)
    col_id = lax.broadcasted_iota(jnp.int32, square, 1).astype(f32)
    dst_row = jnp.broadcast_to(dst, square)
    dst_col = jnp.transpose(dst_row)
    src_col = jnp.transpose(jnp.broadcast_to(src, square))
    rank = jnp.sum(jnp.where((dst_row == dst_col) & (row_id < col_id), 1.0, 0.0), axis=0, keepdims=True)
    many_col = jnp.sum(jnp.where(dst_row == row_id, 1.0, 0.0)[:16], axis=1, keepdims=True)
    many_row = jnp.sum(jnp.where(dst_col == col_id, 1.0, 0.0), axis=0, keepdims=True)
    pairs_col = jnp.floor((many_col + 1.0) * 0.5)
    pairs_row = jnp.where(lane < 16, jnp.floor((many_row + 1.0) * 0.5), 0.0)
    few_row, few_col = row_id[:16], col_id[:16]
    start_col = jnp.sum(jnp.where(few_col < few_row, pairs_row, 0.0), axis=1, keepdims=True)
    before = jnp.sum(jnp.where(few_row < dst, pairs_col, 0.0), axis=0, keepdims=True)
    place = jnp.where(live, 2.0 * before + rank, -1.0)
    hit = jnp.where(jnp.transpose(jnp.broadcast_to(place, square)) == col_id, 1.0, 0.0)
    offs = jnp.where(lane < 16, 4.0 * slot_rows + HEAD + PACK * lane.astype(f32), 0.0)[:, :LANES]
    short = lane[:, :LANES]
    for d in range(PEERS):
        spot = 4 - offset(d)
        table = g_ref[spot, :HEAD, :].astype(f32)[d:d + 1]
        block = table
        if spot in (0, 8):
            block = jnp.where(core == spot // 8, short.astype(f32), table)
        first = jnp.where(short.astype(f32) < table[:, SLOTS:SLOTS + 1], float(spot * slot_rows + HEAD) + PACK * block,
                          float(zero_row))
        first = jnp.where(short < SLOTS, first, 0.0)
        offs = offs + pltpu.roll(jnp.broadcast_to(first, (8, LANES)), 16 + SLOTS * d, 1)[:1]
    offs = jnp.concatenate([offs, jnp.zeros((1, LANES), f32)], axis=1)
    from_col = jnp.sum(jnp.where(src_col == col_id, offs, 0.0), axis=1, keepdims=True)
    opens = jnp.sum(jnp.where((start_col == few_col) & (pairs_col > 0.0), 1.0, 0.0), axis=0, keepdims=True)
    ends = jnp.sum(jnp.where(few_row <= few_col, pairs_col, 0.0), axis=0, keepdims=True)
    rows = (
        jnp.sum(hit * row_id, axis=0, keepdims=True),
        jnp.sum(hit * (from_col - zero_row), axis=0, keepdims=True) + zero_row,
        jnp.sum(hit, axis=0, keepdims=True),
        1.0 - opens,
        jnp.where(pairs_row > 0.0, ends, 0.0),
    )
    for k, row in enumerate(rows):
        idx_ref[k:k + 1, :] = row.astype(jnp.int32)


def exchange(layer, count_ref, h_ref, list_ref, many_ref, ws_ref, wn_ref, b_ref, dst_ref, src_ref, g_ref, s_ref, idx_ref,
             held, lhs, raw, w_ref, picked, tab, load_sem, raw_sem, ysend, yrecv, xsend, xrecv, psend, precv):
    i = lax.axis_index("dom")
    y = lax.axis_index("feat")
    n_dom = lax.axis_size("dom")
    core = lax.rem(i, 2)
    y_up, y_down = lax.rem(y + 1, 4), lax.rem(y + 3, 4)
    x_up, x_down = lax.rem(i + 2, n_dom), lax.rem(i + n_dom - 2, n_dom)
    partner = i + 1 - 2 * core
    NC = len(CHUNKS)
    first_row = [sum(CHUNKS[:n]) * PACK for n in range(NC)]

    def hrows(n, part=None):
        size = CHUNKS[n] * PACK
        if part is None:
            return pl.ds(first_row[n], size)
        return pl.ds(first_row[n] + part * (size // 2), size // 2)

    def grows(n):
        size = CHUNKS[n] * PACK
        return pl.ds(0, HEAD + size) if n == 0 else pl.ds(HEAD + first_row[n], size)

    def remote(src, dst, send, recv, dom, feat):
        return pltpu.make_async_remote_copy(
            src_ref=src, dst_ref=dst, send_sem=send, recv_sem=recv,
            device_id=(dom, feat), device_id_type=MESH)

    loads = [pltpu.make_async_copy(h_ref.at[hrows(n)], held.at[y, hrows(n)], load_sem.at[n]) for n in range(NC)]
    for load in loads:
        load.start()
    window = pl.ds(pl.multiple_of((3 * y // 2) * LANES, LANES), 2 * LANES)
    raws = [pltpu.make_async_copy(ref.at[layer, :, window], raw.at[k], raw_sem.at[k]) for k, ref in enumerate((wn_ref, ws_ref))]
    for load in raws:
        load.start()

    barrier = pltpu.get_barrier_semaphore()
    for dom, feat in ((i, y_up), (i, y_down), (x_up, y), (x_down, y), (partner, y)):
        pl.semaphore_signal(barrier, inc=1, device_id=(dom, feat), device_id_type=MESH)
    pl.semaphore_wait(barrier, 5)

    sent = []
    up, down = [], []

    def gather_own(n):
        loads[n].wait()
        a = remote(held.at[y, hrows(n)], held.at[y, hrows(n)], ysend.at[0, n], yrecv.at[0, n], i, y_up)
        b = remote(held.at[y, hrows(n)], held.at[y, hrows(n)], ysend.at[1, n], yrecv.at[1, n], i, y_down)
        a.start()
        b.start()
        up.append(a)
        down.append(b)
        sent.extend([a, b])

    for n in range(min(AHEAD, NC)):
        gather_own(n)

    def gather_relay(n):
        up[n].wait_recv()
        a = remote(held.at[y_down, hrows(n, 0)], held.at[y_down, hrows(n, 0)], ysend.at[2, n], yrecv.at[2, n], i, y_up)
        a.start()
        down[n].wait_recv()
        b = remote(held.at[y_up, hrows(n, 1)], held.at[y_up, hrows(n, 1)], ysend.at[3, n], yrecv.at[3, n], i, y_down)
        b.start()
        sent.extend([a, b])
        if n + AHEAD < NC:
            gather_own(n + AHEAD)
        return a, b

    lane = lax.broadcasted_iota(jnp.int32, (64, LANES), 1)
    low = lane < 64

    def project(n):
        blocks = CHUNKS[n]
        for j in range(blocks):
            base = first_row[n] + j * PACK
            out = slice(j * BLK, (j + 1) * BLK)
            top = slice(j * BLK, j * BLK + 64)
            bot = slice(j * BLK + 64, (j + 1) * BLK)
            for a in range(4):
                lhs[out, a * LANES:(a + 1) * LANES] = held[a, base:base + BLK, :]
            for pair in range(2):
                p0 = held[2 * pair, base + BLK:base + PACK, :]
                p1 = held[2 * pair + 1, base + BLK:base + PACK, :]
                cols = slice(512 + pair * LANES, 512 + (pair + 1) * LANES)
                lhs[top, cols] = jnp.concatenate([p0[:, :64], p1[:, :64]], axis=1)
                lhs[bot, cols] = jnp.concatenate([p0[:, 64:], p1[:, 64:]], axis=1)
        res = jnp.dot(lhs[:blocks * BLK], w_ref[...], preferred_element_type=jnp.float32) + bias
        for j in range(blocks):
            r0 = j * BLK
            base = first_row[n] + j * PACK
            g_ref[4, HEAD + base:HEAD + base + BLK, :] = res[r0:r0 + BLK, :LANES].astype(jnp.bfloat16)
            s_ref[base:base + BLK, :] = res[r0:r0 + BLK, LANES:2 * LANES]
            top = res[r0:r0 + 64, 2 * LANES:]
            bot = res[r0 + 64:r0 + BLK, 2 * LANES:]
            g_ref[4, HEAD + base + BLK:HEAD + base + PACK, :] = jnp.where(
                low, top, pltpu.roll(bot, 64, 1)).astype(jnp.bfloat16)
            s_ref[base + BLK:base + PACK, :] = jnp.where(low, pltpu.roll(top, 64, 1), bot)

    whole_to = x_down + core * (x_up - x_down)
    whole_from, whole_at = 6 - 4 * core, 8 - 8 * core
    list_to = x_up + core * (x_down - x_up)
    list_from, list_at = 2 + 4 * core, 8 * core
    ours, first, second, listed = [], [], [], []

    def group(m):
        size = sum(CHUNKS) // GROUPS * PACK
        return pl.ds(0, HEAD + size) if m == 0 else pl.ds(HEAD + m * size, size)

    def send_own(n):
        src = g_ref.at[4, grows(n)]
        a = remote(src, g_ref.at[2, grows(n)], xsend.at[0, n], xrecv.at[0, n], x_up, y)
        b = remote(src, g_ref.at[6, grows(n)], xsend.at[1, n], xrecv.at[1, n], x_down, y)
        c = remote(src, g_ref.at[3 + 2 * core, grows(n)], psend.at[0, n], precv.at[0, n], partner, y)
        for copy in (a, b, c):
            copy.start()
        ours.append((a, b, c))
        sent.extend([a, b, c])

    def relay_group(m):
        per = NC // GROUPS
        for n in range(m * per, (m + 1) * per):
            ours[n][0].wait_recv()
            ours[n][1].wait_recv()
        u = remote(g_ref.at[whole_from, group(m)], g_ref.at[whole_at, group(m)], xsend.at[2, m], xrecv.at[2, m], whole_to, y)
        pu = remote(g_ref.at[2, group(m)], g_ref.at[1 + 2 * core, group(m)], psend.at[1, m], precv.at[1, m], partner, y)
        pv = remote(g_ref.at[6, group(m)], g_ref.at[5 + 2 * core, group(m)], psend.at[2, m], precv.at[2, m], partner, y)
        for copy in (u, pu, pv):
            copy.start()
        first.append((u, pu, pv))
        sent.extend([u, pu, pv])

    def relay_list():
        picked[:HEAD, :] = g_ref[list_from, :HEAD, :]
        table = g_ref[list_from, :HEAD, :].astype(jnp.float32)
        wanted = jnp.where(core == 1, table[7:8], table[6:7])
        short = lax.broadcasted_iota(jnp.int32, (1, LANES), 1)

        def pick(s, carry):
            block = jnp.sum(jnp.where(short == s, wanted, 0.0), axis=1, keepdims=True)
            block = jnp.broadcast_to(block, (16, LANES))
            total = jnp.zeros((PACK // 16, 16, LANES), jnp.bfloat16)
            for j in range(sum(CHUNKS)):
                one = jnp.where(block == float(j), 1.0, 0.0).astype(jnp.bfloat16)
                rows = g_ref[list_from, HEAD + j * PACK:HEAD + (j + 1) * PACK, :]
                total = total + rows.reshape(PACK // 16, 16, LANES) * one[None]
            picked[pl.ds(pl.multiple_of(HEAD + s * PACK, 16), PACK), :] = total.reshape(PACK, LANES)
            return carry

        lax.fori_loop(0, SLOTS, pick, 0)
        copy = remote(picked, g_ref.at[list_at, pl.ds(0, HEAD + SLOTS * PACK)], xsend.at[3, 0], xrecv.at[3, 0], list_to, y)
        copy.start()
        listed.append(copy)
        sent.append(copy)

    def relay_two(m):
        first[m][0].wait_recv()
        c = remote(g_ref.at[whole_at, group(m)], g_ref.at[7 - 6 * core, group(m)], psend.at[3, m], precv.at[3, m], partner, y)
        c.start()
        second.append(c)
        sent.append(c)

    g_ref[PLACES, :PACK, :] = jnp.zeros((PACK, LANES), jnp.bfloat16)
    odd = lax.rem(y, 2) == 1
    for load in raws:
        load.wait()
    n_first, n_rest = cut(raw[0], odd)
    s_first, s_rest = cut(raw[1], odd)
    rest = jnp.concatenate([n_rest, s_rest], axis=1)
    for a in range(4):
        for part, cols in ((n_first, 0), (s_first, 1), (rest, 2)):
            cols = slice(cols * LANES, (cols + 1) * LANES)
            w_ref[a * BLK:(a + 1) * BLK, cols] = part[a * PACK:a * PACK + BLK]
            w_ref[512 + a * 64:512 + (a + 1) * 64, cols] = part[a * PACK + BLK:(a + 1) * PACK]
    b_first, b_rest = cut(b_ref[layer:layer + 1, window], odd)
    bias = jnp.concatenate([jnp.zeros((1, LANES), jnp.float32), b_first, jnp.zeros((1, 64), jnp.float32), b_rest], axis=1)

    tab[...] = jnp.zeros(tab.shape, jnp.float32)
    tab[:PEERS, :SLOTS] = list_ref[...].astype(jnp.float32)
    diagonal = lax.broadcasted_iota(jnp.int32, (PEERS, PEERS), 0) == lax.broadcasted_iota(jnp.int32, (PEERS, PEERS), 1)
    many = jnp.where(diagonal, many_ref[...].astype(jnp.float32), 0.0)
    tab[:PEERS, SLOTS:SLOTS + 1] = jnp.sum(many, axis=1, keepdims=True)
    g_ref[4, :HEAD, :] = tab[...].astype(jnp.bfloat16)

    relays = [gather_relay(0)]
    for n in range(NC):
        for relay in relays[n]:
            relay.wait_recv()
        project(n)
        send_own(n)
        if n + 1 < NC:
            relays.append(gather_relay(n + 1))
        for m in range(GROUPS):
            if n == min((m + 1) * (NC // GROUPS), NC - 1):
                relay_group(m)
    relay_list()
    for m in range(GROUPS):
        relay_two(m)
    for n in range(NC):
        ours[n][2].wait_recv()
    for m in range(GROUPS):
        first[m][1].wait_recv()
        first[m][2].wait_recv()
        second[m].wait_recv()
    listed[0].wait_recv()
    if layer == 0:
        order_tiles(count_ref[0], dst_ref[...], src_ref[...], core, g_ref, idx_ref)
    else:
        idx_ref[...] = jnp.zeros(idx_ref.shape, idx_ref.dtype)
    for copy in sent:
        copy.wait_send()


def aggregate(last, idx, gv, tv, s_ref, out_ref, part):
    lane = lax.broadcasted_iota(jnp.int32, (64, LANES), 1)
    low = lane < 64

    def source(q):
        row = pl.multiple_of(idx[1, q], 16)
        ones = jnp.full((64, 64), idx[2, q].astype(jnp.float32)).astype(jnp.bfloat16)
        left = gv[pl.ds(row, BLK), :]
        pack = gv[pl.ds(row + BLK, 64), :]
        right = jnp.concatenate([
            jnp.concatenate([pack[:, :64], ones], axis=1),
            jnp.concatenate([pack[:, 64:], ones], axis=1),
        ], axis=0)
        return jnp.concatenate([left, right], axis=1)

    def product(p):
        q = 2 * p
        lhs = jnp.concatenate([tv[idx[0, q]], tv[idx[0, q + 1]]], axis=1)
        rhs = jnp.concatenate([source(q), source(q + 1)], axis=0)
        return jnp.dot(lhs, rhs, preferred_element_type=jnp.float32)

    part[0] = jnp.zeros(part.shape[1:], jnp.float32)

    def step(g, carry):
        products = [product(g * UNROLL + u) for u in range(UNROLL)]
        for u in range(UNROLL):
            p = g * UNROLL + u
            part[p + 1] = part[p] * idx[3, p].astype(jnp.float32) + products[u]
        return carry

    lax.fori_loop(0, (part.shape[0] - 1) // UNROLL, step, 0)

    for b in range(s_ref.shape[0] // PACK):
        acc = part[idx[4, b]]
        scale = 1.0 / (1.0 + acc[:, PACK:PACK + 1])
        left = acc[:, :LANES] * scale
        right = acc[:, LANES:] * scale
        pack = jnp.where(low, right[:64], pltpu.roll(right[64:], 64, 1))
        base = b * PACK
        left = left + s_ref[base:base + BLK, :]
        pack = pack + s_ref[base + BLK:base + PACK, :]
        if last:
            row = b * BLK
            out_ref[row:row + BLK, :LANES] = left.astype(jnp.bfloat16)
            out_ref[row:row + 64, LANES:] = pack[:, :64].astype(jnp.bfloat16)
            out_ref[row + 64:row + BLK, LANES:] = pltpu.roll(pack, 64, 1)[:, :64].astype(jnp.bfloat16)
        else:
            out_ref[base:base + BLK, :] = jnp.maximum(left, 0.0).astype(jnp.bfloat16)
            out_ref[base + BLK:base + PACK, :] = jnp.maximum(pack, 0.0).astype(jnp.bfloat16)


def per_device(
    feats, tile_vals, tile_dst, tile_src, tile_count, send_blocks, send_count, w_self, w_nbr, bias
):
    node_rows, cols = feats.shape
    blk_dev = node_rows // BLK
    packed_rows = blk_dev * PACK
    slot_rows = HEAD + packed_rows
    tiles = tile_vals.shape[0]
    entries = tiles + blk_dev

    f3 = feats.reshape(blk_dev, BLK, cols)
    hidden = jnp.concatenate(
        [f3[..., :128], jnp.concatenate([f3[:, :64, 128:], f3[:, 64:, 128:]], axis=2)], axis=1
    ).reshape(packed_rows, LANES)

    NC = len(CHUNKS)
    vmem = pl.BlockSpec(memory_space=pltpu.VMEM)
    anywhere = pl.BlockSpec(memory_space=pl.ANY)
    hbm = pl.BlockSpec(memory_space=pltpu.HBM)

    def exchange_call(layer):
        return pl.pallas_call(
            functools.partial(exchange, layer),
            out_shape=(
                jax.ShapeDtypeStruct((PLACES + 1, slot_rows, LANES), jnp.bfloat16),
                jax.ShapeDtypeStruct((packed_rows, LANES), jnp.float32),
                jax.ShapeDtypeStruct((8, 2 * LANES), jnp.int32),
            ),
            in_specs=[pl.BlockSpec(memory_space=pltpu.SMEM), anywhere, vmem, vmem, hbm, hbm, vmem, vmem, vmem],
            out_specs=(vmem, vmem, vmem),
            scratch_shapes=[
                pltpu.VMEM((4, packed_rows, LANES), jnp.bfloat16),
                pltpu.VMEM((max(CHUNKS) * BLK, 768), jnp.bfloat16),
                pltpu.VMEM((2, 768, 2 * LANES), jnp.bfloat16),
                pltpu.VMEM((768, 3 * LANES), jnp.bfloat16),
                pltpu.VMEM((HEAD + SLOTS * PACK, LANES), jnp.bfloat16),
                pltpu.VMEM((HEAD, LANES), jnp.float32),
                pltpu.SemaphoreType.DMA((NC,)),
                pltpu.SemaphoreType.DMA((2,)),
            ] + [pltpu.SemaphoreType.DMA((4, NC)) for _ in range(6)],
            compiler_params=pltpu.CompilerParams(
                collective_id=layer, has_side_effects=True, vmem_limit_bytes=EXCHANGE_BYTES
            ),
            name=f"exchange{layer}",
        )

    def aggregate_call(last):
        out = (node_rows, cols) if last else (packed_rows, LANES)
        return pl.pallas_call(
            functools.partial(aggregate, last),
            out_shape=jax.ShapeDtypeStruct(out, jnp.bfloat16),
            grid_spec=pltpu.PrefetchScalarGridSpec(
                num_scalar_prefetch=1,
                grid=(),
                in_specs=[vmem, vmem, vmem],
                out_specs=vmem,
                scratch_shapes=[pltpu.VMEM((entries // 2 + 1, BLK, 2 * LANES), jnp.float32)],
            ),
            compiler_params=pltpu.CompilerParams(vmem_limit_bytes=AGGREGATE_BYTES),
            name="aggregate_last" if last else "aggregate",
        )

    dsts, srcs = tile_dst[None, :], tile_src[None, :]
    ws, wn = (pltpu.with_memory_space_constraint(w, pltpu.HBM) for w in (w_self, w_nbr))
    for layer in range(LAYERS):
        g, s, order = exchange_call(layer)(tile_count, hidden, send_blocks[0], send_count, ws, wn, bias, dsts, srcs)
        idx = order if layer == 0 else idx
        g = g.reshape((PLACES + 1) * slot_rows, LANES)
        hidden = aggregate_call(layer == LAYERS - 1)(idx, g, tile_vals, s)
    return hidden


def solution(mesh):
    in_specs = (
        P("dom", "feat"),
        P("dom", None, None),
        P("dom"),
        P("dom"),
        P("dom"),
        P("dom", None, None),
        P("dom", None),
        P(),
        P(),
        P(),
    )
    out_specs = P("dom", "feat")
    return jax.shard_map(
        per_device, mesh=mesh, in_specs=in_specs, out_specs=out_specs, check_vma=False
    )
```

```python
import functools

import jax
import jax.numpy as jnp
from jax import lax
from jax.experimental import pallas as pl
from jax.experimental.pallas import tpu as pltpu
from jax.sharding import PartitionSpec as P

LAYERS = 3
BLK = 128
PEERS = 8
SLOTS = 8
MESH = pl.DeviceIdType.MESH
LANES = 128
PACK = 192
HEAD = 16
CHUNKS = (4, 4, 4, 4)
GROUPS = 4
AHEAD = 2
PLACES = 9
UNROLL = 26
EXCHANGE_BYTES = 14 * 1024 * 1024
AGGREGATE_BYTES = 17 * 1024 * 1024


def offset(d):
    return (d // 2 + 1) * (1 if d % 2 == 0 else -1)


def cut(raw, odd):
    t0, t1 = raw[:, :128], raw[:, 128:]
    first = jnp.where(odd, jnp.concatenate([t0[:, 64:], t1[:, :64]], axis=1), t0)
    rest = jnp.where(odd, t1[:, 64:], t1[:, :64])
    return first, rest


def order_tiles(count, dst, src, core, g_ref, idx_ref):
    f32 = jnp.float32
    wide = 2 * LANES
    slot_rows = g_ref.shape[1]
    zero_row = PLACES * slot_rows
    tiles = dst.shape[1]
    pad = jnp.zeros((1, wide - tiles), f32)
    lane = lax.broadcasted_iota(jnp.int32, (1, wide), 1)
    live = lane < count
    dst = jnp.where(live, jnp.concatenate([dst.astype(f32), pad], axis=1), float(wide))
    src = jnp.concatenate([src.astype(f32), pad], axis=1)
    square = (wide, wide)
    row_id = lax.broadcasted_iota(jnp.int32, square, 0).astype(f32)
    col_id = lax.broadcasted_iota(jnp.int32, square, 1).astype(f32)
    dst_row = jnp.broadcast_to(dst, square)
    dst_col = jnp.transpose(dst_row)
    src_col = jnp.transpose(jnp.broadcast_to(src, square))
    rank = jnp.sum(jnp.where((dst_row == dst_col) & (row_id < col_id), 1.0, 0.0), axis=0, keepdims=True)
    many_col = jnp.sum(jnp.where(dst_row == row_id, 1.0, 0.0)[:16], axis=1, keepdims=True)
    many_row = jnp.sum(jnp.where(dst_col == col_id, 1.0, 0.0), axis=0, keepdims=True)
    pairs_col = jnp.floor((many_col + 1.0) * 0.5)
    pairs_row = jnp.where(lane < 16, jnp.floor((many_row + 1.0) * 0.5), 0.0)
    few_row, few_col = row_id[:16], col_id[:16]
    start_col = jnp.sum(jnp.where(few_col < few_row, pairs_row, 0.0), axis=1, keepdims=True)
    before = jnp.sum(jnp.where(few_row < dst, pairs_col, 0.0), axis=0, keepdims=True)
    place = jnp.where(live, 2.0 * before + rank, -1.0)
    hit = jnp.where(jnp.transpose(jnp.broadcast_to(place, square)) == col_id, 1.0, 0.0)
    offs = jnp.where(lane < 16, 4.0 * slot_rows + HEAD + PACK * lane.astype(f32), 0.0)[:, :LANES]
    short = lane[:, :LANES]
    for d in range(PEERS):
        spot = 4 - offset(d)
        table = g_ref[spot, :HEAD, :].astype(f32)[d:d + 1]
        block = table
        if spot in (0, 8):
            block = jnp.where(core == spot // 8, short.astype(f32), table)
        first = jnp.where(short.astype(f32) < table[:, SLOTS:SLOTS + 1], float(spot * slot_rows + HEAD) + PACK * block,
                          float(zero_row))
        first = jnp.where(short < SLOTS, first, 0.0)
        offs = offs + pltpu.roll(jnp.broadcast_to(first, (8, LANES)), 16 + SLOTS * d, 1)[:1]
    offs = jnp.concatenate([offs, jnp.zeros((1, LANES), f32)], axis=1)
    from_col = jnp.sum(jnp.where(src_col == col_id, offs, 0.0), axis=1, keepdims=True)
    opens = jnp.sum(jnp.where((start_col == few_col) & (pairs_col > 0.0), 1.0, 0.0), axis=0, keepdims=True)
    ends = jnp.sum(jnp.where(few_row <= few_col, pairs_col, 0.0), axis=0, keepdims=True)
    rows = (
        jnp.sum(hit * row_id, axis=0, keepdims=True),
        jnp.sum(hit * (from_col - zero_row), axis=0, keepdims=True) + zero_row,
        jnp.sum(hit, axis=0, keepdims=True),
        1.0 - opens,
        jnp.where(pairs_row > 0.0, ends, 0.0),
    )
    for k, row in enumerate(rows):
        idx_ref[k:k + 1, :] = row.astype(jnp.int32)


def exchange(layer, count_ref, h_ref, list_ref, many_ref, ws_ref, wn_ref, b_ref, dst_ref, src_ref, g_ref, s_ref, idx_ref,
             held, lhs, raw, w_ref, picked, tab, load_sem, raw_sem, ysend, yrecv, xsend, xrecv, psend, precv):
    i = lax.axis_index("dom")
    y = lax.axis_index("feat")
    n_dom = lax.axis_size("dom")
    core = lax.rem(i, 2)
    y_up, y_down = lax.rem(y + 1, 4), lax.rem(y + 3, 4)
    x_up, x_down = lax.rem(i + 2, n_dom), lax.rem(i + n_dom - 2, n_dom)
    partner = i + 1 - 2 * core
    NC = len(CHUNKS)
    first_row = [sum(CHUNKS[:n]) * PACK for n in range(NC)]

    def hrows(n, part=None):
        size = CHUNKS[n] * PACK
        if part is None:
            return pl.ds(first_row[n], size)
        return pl.ds(first_row[n] + part * (size // 2), size // 2)

    def grows(n):
        size = CHUNKS[n] * PACK
        return pl.ds(0, HEAD + size) if n == 0 else pl.ds(HEAD + first_row[n], size)

    def remote(src, dst, send, recv, dom, feat):
        return pltpu.make_async_remote_copy(
            src_ref=src, dst_ref=dst, send_sem=send, recv_sem=recv,
            device_id=(dom, feat), device_id_type=MESH)

    loads = [pltpu.make_async_copy(h_ref.at[hrows(n)], held.at[y, hrows(n)], load_sem.at[n]) for n in range(NC)]
    for load in loads:
        load.start()
    window = pl.ds(pl.multiple_of((3 * y // 2) * LANES, LANES), 2 * LANES)
    raws = [pltpu.make_async_copy(ref.at[layer, :, window], raw.at[k], raw_sem.at[k]) for k, ref in enumerate((wn_ref, ws_ref))]
    for load in raws:
        load.start()

    barrier = pltpu.get_barrier_semaphore()
    for dom, feat in ((i, y_up), (i, y_down), (x_up, y), (x_down, y), (partner, y)):
        pl.semaphore_signal(barrier, inc=1, device_id=(dom, feat), device_id_type=MESH)
    pl.semaphore_wait(barrier, 5)

    sent = []
    up, down = [], []

    def gather_own(n):
        loads[n].wait()
        a = remote(held.at[y, hrows(n)], held.at[y, hrows(n)], ysend.at[0, n], yrecv.at[0, n], i, y_up)
        b = remote(held.at[y, hrows(n)], held.at[y, hrows(n)], ysend.at[1, n], yrecv.at[1, n], i, y_down)
        a.start()
        b.start()
        up.append(a)
        down.append(b)
        sent.extend([a, b])

    for n in range(min(AHEAD, NC)):
        gather_own(n)

    def gather_relay(n):
        up[n].wait_recv()
        a = remote(held.at[y_down, hrows(n, 0)], held.at[y_down, hrows(n, 0)], ysend.at[2, n], yrecv.at[2, n], i, y_up)
        a.start()
        down[n].wait_recv()
        b = remote(held.at[y_up, hrows(n, 1)], held.at[y_up, hrows(n, 1)], ysend.at[3, n], yrecv.at[3, n], i, y_down)
        b.start()
        sent.extend([a, b])
        if n + AHEAD < NC:
            gather_own(n + AHEAD)
        return a, b

    lane = lax.broadcasted_iota(jnp.int32, (64, LANES), 1)
    low = lane < 64

    def project(n):
        blocks = CHUNKS[n]
        for j in range(blocks):
            base = first_row[n] + j * PACK
            out = slice(j * BLK, (j + 1) * BLK)
            top = slice(j * BLK, j * BLK + 64)
            bot = slice(j * BLK + 64, (j + 1) * BLK)
            for a in range(4):
                lhs[out, a * LANES:(a + 1) * LANES] = held[a, base:base + BLK, :]
            for pair in range(2):
                p0 = held[2 * pair, base + BLK:base + PACK, :]
                p1 = held[2 * pair + 1, base + BLK:base + PACK, :]
                cols = slice(512 + pair * LANES, 512 + (pair + 1) * LANES)
                lhs[top, cols] = jnp.concatenate([p0[:, :64], p1[:, :64]], axis=1)
                lhs[bot, cols] = jnp.concatenate([p0[:, 64:], p1[:, 64:]], axis=1)
        res = jnp.dot(lhs[:blocks * BLK], w_ref[...], preferred_element_type=jnp.float32) + bias
        for j in range(blocks):
            r0 = j * BLK
            base = first_row[n] + j * PACK
            g_ref[4, HEAD + base:HEAD + base + BLK, :] = res[r0:r0 + BLK, :LANES].astype(jnp.bfloat16)
            s_ref[base:base + BLK, :] = res[r0:r0 + BLK, LANES:2 * LANES]
            top = res[r0:r0 + 64, 2 * LANES:]
            bot = res[r0 + 64:r0 + BLK, 2 * LANES:]
            g_ref[4, HEAD + base + BLK:HEAD + base + PACK, :] = jnp.where(
                low, top, pltpu.roll(bot, 64, 1)).astype(jnp.bfloat16)
            s_ref[base + BLK:base + PACK, :] = jnp.where(low, pltpu.roll(top, 64, 1), bot)

    whole_to = x_down + core * (x_up - x_down)
    whole_from, whole_at = 6 - 4 * core, 8 - 8 * core
    list_to = x_up + core * (x_down - x_up)
    list_from, list_at = 2 + 4 * core, 8 * core
    ours, first, second, listed = [], [], [], []

    def group(m):
        size = sum(CHUNKS) // GROUPS * PACK
        return pl.ds(0, HEAD + size) if m == 0 else pl.ds(HEAD + m * size, size)

    def send_own(n):
        src = g_ref.at[4, grows(n)]
        a = remote(src, g_ref.at[2, grows(n)], xsend.at[0, n], xrecv.at[0, n], x_up, y)
        b = remote(src, g_ref.at[6, grows(n)], xsend.at[1, n], xrecv.at[1, n], x_down, y)
        c = remote(src, g_ref.at[3 + 2 * core, grows(n)], psend.at[0, n], precv.at[0, n], partner, y)
        for copy in (a, b, c):
            copy.start()
        ours.append((a, b, c))
        sent.extend([a, b, c])

    def relay_group(m):
        per = NC // GROUPS
        for n in range(m * per, (m + 1) * per):
            ours[n][0].wait_recv()
            ours[n][1].wait_recv()
        u = remote(g_ref.at[whole_from, group(m)], g_ref.at[whole_at, group(m)], xsend.at[2, m], xrecv.at[2, m], whole_to, y)
        pu = remote(g_ref.at[2, group(m)], g_ref.at[1 + 2 * core, group(m)], psend.at[1, m], precv.at[1, m], partner, y)
        pv = remote(g_ref.at[6, group(m)], g_ref.at[5 + 2 * core, group(m)], psend.at[2, m], precv.at[2, m], partner, y)
        u.start()
        if m < GROUPS - 1:
            pu.start()
            pv.start()
        first.append((u, pu, pv))
        sent.extend([u, pu, pv])

    def pick_blocks(low_block, high_block):
        table = g_ref[list_from, :HEAD, :].astype(jnp.float32)
        wanted = jnp.where(core == 1, table[7:8], table[6:7])
        short = lax.broadcasted_iota(jnp.int32, (1, LANES), 1)

        def pick(s, carry):
            block = jnp.sum(jnp.where(short == s, wanted, 0.0), axis=1, keepdims=True)
            block = jnp.broadcast_to(block, (16, LANES))
            place = pl.ds(pl.multiple_of(HEAD + s * PACK, 16), PACK)
            if low_block == 0:
                total = jnp.zeros((PACK // 16, 16, LANES), jnp.bfloat16)
            else:
                total = picked[place, :].reshape(PACK // 16, 16, LANES)
            for j in range(low_block, high_block):
                one = jnp.where(block == float(j), 1.0, 0.0).astype(jnp.bfloat16)
                rows = g_ref[list_from, HEAD + j * PACK:HEAD + (j + 1) * PACK, :]
                total = total + rows.reshape(PACK // 16, 16, LANES) * one[None]
            picked[place, :] = total.reshape(PACK, LANES)
            return carry

        lax.fori_loop(0, SLOTS, pick, 0)

    def relay_list():
        picked[:HEAD, :] = g_ref[list_from, :HEAD, :]
        pick_blocks(sum(CHUNKS[:-1]), sum(CHUNKS))
        copy = remote(picked, g_ref.at[list_at, pl.ds(0, HEAD + SLOTS * PACK)], xsend.at[3, 0], xrecv.at[3, 0], list_to, y)
        copy.start()
        listed.append(copy)
        sent.append(copy)

    def relay_two(m):
        first[m][0].wait_recv()
        c = remote(g_ref.at[whole_at, group(m)], g_ref.at[7 - 6 * core, group(m)], psend.at[3, m], precv.at[3, m], partner, y)
        c.start()
        second.append(c)
        sent.append(c)

    g_ref[PLACES, :PACK, :] = jnp.zeros((PACK, LANES), jnp.bfloat16)
    odd = lax.rem(y, 2) == 1
    for load in raws:
        load.wait()
    n_first, n_rest = cut(raw[0], odd)
    s_first, s_rest = cut(raw[1], odd)
    rest = jnp.concatenate([n_rest, s_rest], axis=1)
    for a in range(4):
        for part, cols in ((n_first, 0), (s_first, 1), (rest, 2)):
            cols = slice(cols * LANES, (cols + 1) * LANES)
            w_ref[a * BLK:(a + 1) * BLK, cols] = part[a * PACK:a * PACK + BLK]
            w_ref[512 + a * 64:512 + (a + 1) * 64, cols] = part[a * PACK + BLK:(a + 1) * PACK]
    b_first, b_rest = cut(b_ref[layer:layer + 1, window], odd)
    bias = jnp.concatenate([jnp.zeros((1, LANES), jnp.float32), b_first, jnp.zeros((1, 64), jnp.float32), b_rest], axis=1)

    tab[...] = jnp.zeros(tab.shape, jnp.float32)
    tab[:PEERS, :SLOTS] = list_ref[...].astype(jnp.float32)
    diagonal = lax.broadcasted_iota(jnp.int32, (PEERS, PEERS), 0) == lax.broadcasted_iota(jnp.int32, (PEERS, PEERS), 1)
    many = jnp.where(diagonal, many_ref[...].astype(jnp.float32), 0.0)
    tab[:PEERS, SLOTS:SLOTS + 1] = jnp.sum(many, axis=1, keepdims=True)
    g_ref[4, :HEAD, :] = tab[...].astype(jnp.bfloat16)

    relays = [gather_relay(0)]
    for n in range(NC):
        for relay in relays[n]:
            relay.wait_recv()
        project(n)
        send_own(n)
        if n + 1 < NC:
            relays.append(gather_relay(n + 1))
        for m in range(GROUPS):
            if n == min((m + 1) * (NC // GROUPS), NC - 1):
                relay_group(m)
                if m == GROUPS - 2:
                    pick_blocks(0, sum(CHUNKS[:-1]))
    relay_list()
    first[-1][1].start()
    first[-1][2].start()
    for m in range(GROUPS):
        relay_two(m)
    for n in range(NC):
        ours[n][2].wait_recv()
    for m in range(GROUPS):
        first[m][1].wait_recv()
        first[m][2].wait_recv()
        second[m].wait_recv()
    listed[0].wait_recv()
    if layer == 0:
        order_tiles(count_ref[0], dst_ref[...], src_ref[...], core, g_ref, idx_ref)
    else:
        idx_ref[...] = jnp.zeros(idx_ref.shape, idx_ref.dtype)
    for copy in sent:
        copy.wait_send()


def aggregate(last, idx, gv, tv, s_ref, out_ref, part):
    lane = lax.broadcasted_iota(jnp.int32, (64, LANES), 1)
    low = lane < 64

    def source(q):
        row = pl.multiple_of(idx[1, q], 16)
        ones = jnp.full((64, 64), idx[2, q].astype(jnp.float32)).astype(jnp.bfloat16)
        left = gv[pl.ds(row, BLK), :]
        pack = gv[pl.ds(row + BLK, 64), :]
        right = jnp.concatenate([
            jnp.concatenate([pack[:, :64], ones], axis=1),
            jnp.concatenate([pack[:, 64:], ones], axis=1),
        ], axis=0)
        return jnp.concatenate([left, right], axis=1)

    def product(p):
        q = 2 * p
        lhs = jnp.concatenate([tv[idx[0, q]], tv[idx[0, q + 1]]], axis=1)
        rhs = jnp.concatenate([source(q), source(q + 1)], axis=0)
        return jnp.dot(lhs, rhs, preferred_element_type=jnp.float32)

    part[0] = jnp.zeros(part.shape[1:], jnp.float32)

    def step(g, carry):
        products = [product(g * UNROLL + u) for u in range(UNROLL)]
        for u in range(UNROLL):
            p = g * UNROLL + u
            part[p + 1] = part[p] * idx[3, p].astype(jnp.float32) + products[u]
        return carry

    lax.fori_loop(0, (part.shape[0] - 1) // UNROLL, step, 0)

    for b in range(s_ref.shape[0] // PACK):
        acc = part[idx[4, b]]
        scale = 1.0 / (1.0 + acc[:, PACK:PACK + 1])
        left = acc[:, :LANES] * scale
        right = acc[:, LANES:] * scale
        pack = jnp.where(low, right[:64], pltpu.roll(right[64:], 64, 1))
        base = b * PACK
        left = left + s_ref[base:base + BLK, :]
        pack = pack + s_ref[base + BLK:base + PACK, :]
        if last:
            row = b * BLK
            out_ref[row:row + BLK, :LANES] = left.astype(jnp.bfloat16)
            out_ref[row:row + 64, LANES:] = pack[:, :64].astype(jnp.bfloat16)
            out_ref[row + 64:row + BLK, LANES:] = pltpu.roll(pack, 64, 1)[:, :64].astype(jnp.bfloat16)
        else:
            out_ref[base:base + BLK, :] = jnp.maximum(left, 0.0).astype(jnp.bfloat16)
            out_ref[base + BLK:base + PACK, :] = jnp.maximum(pack, 0.0).astype(jnp.bfloat16)


def per_device(
    feats, tile_vals, tile_dst, tile_src, tile_count, send_blocks, send_count, w_self, w_nbr, bias
):
    node_rows, cols = feats.shape
    blk_dev = node_rows // BLK
    packed_rows = blk_dev * PACK
    slot_rows = HEAD + packed_rows
    tiles = tile_vals.shape[0]
    entries = tiles + blk_dev

    f3 = feats.reshape(blk_dev, BLK, cols)
    hidden = jnp.concatenate(
        [f3[..., :128], jnp.concatenate([f3[:, :64, 128:], f3[:, 64:, 128:]], axis=2)], axis=1
    ).reshape(packed_rows, LANES)

    NC = len(CHUNKS)
    vmem = pl.BlockSpec(memory_space=pltpu.VMEM)
    anywhere = pl.BlockSpec(memory_space=pl.ANY)
    hbm = pl.BlockSpec(memory_space=pltpu.HBM)

    def exchange_call(layer):
        return pl.pallas_call(
            functools.partial(exchange, layer),
            out_shape=(
                jax.ShapeDtypeStruct((PLACES + 1, slot_rows, LANES), jnp.bfloat16),
                jax.ShapeDtypeStruct((packed_rows, LANES), jnp.float32),
                jax.ShapeDtypeStruct((8, 2 * LANES), jnp.int32),
            ),
            in_specs=[pl.BlockSpec(memory_space=pltpu.SMEM), anywhere, vmem, vmem, hbm, hbm, vmem, vmem, vmem],
            out_specs=(vmem, vmem, vmem),
            scratch_shapes=[
                pltpu.VMEM((4, packed_rows, LANES), jnp.bfloat16),
                pltpu.VMEM((max(CHUNKS) * BLK, 768), jnp.bfloat16),
                pltpu.VMEM((2, 768, 2 * LANES), jnp.bfloat16),
                pltpu.VMEM((768, 3 * LANES), jnp.bfloat16),
                pltpu.VMEM((HEAD + SLOTS * PACK, LANES), jnp.bfloat16),
                pltpu.VMEM((HEAD, LANES), jnp.float32),
                pltpu.SemaphoreType.DMA((NC,)),
                pltpu.SemaphoreType.DMA((2,)),
            ] + [pltpu.SemaphoreType.DMA((4, NC)) for _ in range(6)],
            compiler_params=pltpu.CompilerParams(
                collective_id=layer, has_side_effects=True, vmem_limit_bytes=EXCHANGE_BYTES
            ),
            name=f"exchange{layer}",
        )

    def aggregate_call(last):
        out = (node_rows, cols) if last else (packed_rows, LANES)
        return pl.pallas_call(
            functools.partial(aggregate, last),
            out_shape=jax.ShapeDtypeStruct(out, jnp.bfloat16),
            grid_spec=pltpu.PrefetchScalarGridSpec(
                num_scalar_prefetch=1,
                grid=(),
                in_specs=[vmem, vmem, vmem],
                out_specs=vmem,
                scratch_shapes=[pltpu.VMEM((entries // 2 + 1, BLK, 2 * LANES), jnp.float32)],
            ),
            compiler_params=pltpu.CompilerParams(vmem_limit_bytes=AGGREGATE_BYTES),
            name="aggregate_last" if last else "aggregate",
        )

    dsts, srcs = tile_dst[None, :], tile_src[None, :]
    ws, wn = (pltpu.with_memory_space_constraint(w, pltpu.HBM) for w in (w_self, w_nbr))
    for layer in range(LAYERS):
        g, s, order = exchange_call(layer)(tile_count, hidden, send_blocks[0], send_count, ws, wn, bias, dsts, srcs)
        idx = order if layer == 0 else idx
        g = g.reshape((PLACES + 1) * slot_rows, LANES)
        hidden = aggregate_call(layer == LAYERS - 1)(idx, g, tile_vals, s)
    return hidden


def solution(mesh):
    in_specs = (
        P("dom", "feat"),
        P("dom", None, None),
        P("dom"),
        P("dom"),
        P("dom"),
        P("dom", None, None),
        P("dom", None),
        P(),
        P(),
        P(),
    )
    out_specs = P("dom", "feat")
    return jax.shard_map(
        per_device, mesh=mesh, in_specs=in_specs, out_specs=out_specs, check_vma=False
    )
```

```python
import functools

import jax
import jax.numpy as jnp
from jax import lax
from jax.experimental import pallas as pl
from jax.experimental.pallas import tpu as pltpu
from jax.sharding import PartitionSpec as P

LAYERS = 3
BLK = 128
PEERS = 8
SLOTS = 8
MESH = pl.DeviceIdType.MESH
LANES = 128
PACK = 192
HEAD = 16
CHUNKS = (4, 4, 4, 4)
GROUPS = 4
AHEAD = 2
PLACES = 9
UNROLL = 52
EXCHANGE_BYTES = 14 * 1024 * 1024
AGGREGATE_BYTES = 22 * 1024 * 1024


def offset(d):
    return (d // 2 + 1) * (1 if d % 2 == 0 else -1)


def cut(raw, odd):
    t0, t1 = raw[:, :128], raw[:, 128:]
    first = jnp.where(odd, jnp.concatenate([t0[:, 64:], t1[:, :64]], axis=1), t0)
    rest = jnp.where(odd, t1[:, 64:], t1[:, :64])
    return first, rest


def order_tiles(count, dst, src, core, g_ref, idx_ref):
    f32 = jnp.float32
    wide = 2 * LANES
    slot_rows = g_ref.shape[1]
    zero_row = PLACES * slot_rows
    tiles = dst.shape[1]
    pad = jnp.zeros((1, wide - tiles), f32)
    lane = lax.broadcasted_iota(jnp.int32, (1, wide), 1)
    live = lane < count
    dst = jnp.where(live, jnp.concatenate([dst.astype(f32), pad], axis=1), float(wide))
    src = jnp.concatenate([src.astype(f32), pad], axis=1)
    square = (wide, wide)
    row_id = lax.broadcasted_iota(jnp.int32, square, 0).astype(f32)
    col_id = lax.broadcasted_iota(jnp.int32, square, 1).astype(f32)
    dst_row = jnp.broadcast_to(dst, square)
    dst_col = jnp.transpose(dst_row)
    src_col = jnp.transpose(jnp.broadcast_to(src, square))
    rank = jnp.sum(jnp.where((dst_row == dst_col) & (row_id < col_id), 1.0, 0.0), axis=0, keepdims=True)
    many_col = jnp.sum(jnp.where(dst_row == row_id, 1.0, 0.0)[:16], axis=1, keepdims=True)
    many_row = jnp.sum(jnp.where(dst_col == col_id, 1.0, 0.0), axis=0, keepdims=True)
    pairs_col = jnp.floor((many_col + 1.0) * 0.5)
    pairs_row = jnp.where(lane < 16, jnp.floor((many_row + 1.0) * 0.5), 0.0)
    few_row, few_col = row_id[:16], col_id[:16]
    start_col = jnp.sum(jnp.where(few_col < few_row, pairs_row, 0.0), axis=1, keepdims=True)
    before = jnp.sum(jnp.where(few_row < dst, pairs_col, 0.0), axis=0, keepdims=True)
    place = jnp.where(live, 2.0 * before + rank, -1.0)
    hit = jnp.where(jnp.transpose(jnp.broadcast_to(place, square)) == col_id, 1.0, 0.0)
    offs = jnp.where(lane < 16, 4.0 * slot_rows + HEAD + PACK * lane.astype(f32), 0.0)[:, :LANES]
    short = lane[:, :LANES]
    for d in range(PEERS):
        spot = 4 - offset(d)
        table = g_ref[spot, :HEAD, :].astype(f32)[d:d + 1]
        block = table
        if spot in (0, 8):
            block = jnp.where(core == spot // 8, short.astype(f32), table)
        first = jnp.where(short.astype(f32) < table[:, SLOTS:SLOTS + 1], float(spot * slot_rows + HEAD) + PACK * block,
                          float(zero_row))
        first = jnp.where(short < SLOTS, first, 0.0)
        offs = offs + pltpu.roll(jnp.broadcast_to(first, (8, LANES)), 16 + SLOTS * d, 1)[:1]
    offs = jnp.concatenate([offs, jnp.zeros((1, LANES), f32)], axis=1)
    from_col = jnp.sum(jnp.where(src_col == col_id, offs, 0.0), axis=1, keepdims=True)
    opens = jnp.sum(jnp.where((start_col == few_col) & (pairs_col > 0.0), 1.0, 0.0), axis=0, keepdims=True)
    ends = jnp.sum(jnp.where(few_row <= few_col, pairs_col, 0.0), axis=0, keepdims=True)
    rows = (
        jnp.sum(hit * row_id, axis=0, keepdims=True),
        jnp.sum(hit * (from_col - zero_row), axis=0, keepdims=True) + zero_row,
        jnp.sum(hit, axis=0, keepdims=True),
        1.0 - opens,
        jnp.where(pairs_row > 0.0, ends, 0.0),
    )
    for k, row in enumerate(rows):
        idx_ref[k:k + 1, :] = row.astype(jnp.int32)


def exchange(layer, count_ref, h_ref, list_ref, many_ref, ws_ref, wn_ref, b_ref, dst_ref, src_ref, g_ref, s_ref, idx_ref,
             held, lhs, raw, w_ref, picked, tab, load_sem, raw_sem, ysend, yrecv, xsend, xrecv, psend, precv):
    i = lax.axis_index("dom")
    y = lax.axis_index("feat")
    n_dom = lax.axis_size("dom")
    core = lax.rem(i, 2)
    y_up, y_down = lax.rem(y + 1, 4), lax.rem(y + 3, 4)
    x_up, x_down = lax.rem(i + 2, n_dom), lax.rem(i + n_dom - 2, n_dom)
    partner = i + 1 - 2 * core
    NC = len(CHUNKS)
    first_row = [sum(CHUNKS[:n]) * PACK for n in range(NC)]

    def hrows(n, part=None):
        size = CHUNKS[n] * PACK
        if part is None:
            return pl.ds(first_row[n], size)
        return pl.ds(first_row[n] + part * (size // 2), size // 2)

    def grows(n):
        size = CHUNKS[n] * PACK
        return pl.ds(0, HEAD + size) if n == 0 else pl.ds(HEAD + first_row[n], size)

    def remote(src, dst, send, recv, dom, feat):
        return pltpu.make_async_remote_copy(
            src_ref=src, dst_ref=dst, send_sem=send, recv_sem=recv,
            device_id=(dom, feat), device_id_type=MESH)

    loads = [pltpu.make_async_copy(h_ref.at[hrows(n)], held.at[y, hrows(n)], load_sem.at[n]) for n in range(NC)]
    for load in loads:
        load.start()
    window = pl.ds(pl.multiple_of((3 * y // 2) * LANES, LANES), 2 * LANES)
    raws = [pltpu.make_async_copy(ref.at[layer, :, window], raw.at[k], raw_sem.at[k]) for k, ref in enumerate((wn_ref, ws_ref))]
    for load in raws:
        load.start()

    barrier = pltpu.get_barrier_semaphore()
    for dom, feat in ((i, y_up), (i, y_down), (x_up, y), (x_down, y), (partner, y)):
        pl.semaphore_signal(barrier, inc=1, device_id=(dom, feat), device_id_type=MESH)
    pl.semaphore_wait(barrier, 5)

    sent = []
    up, down = [], []

    def gather_own(n):
        loads[n].wait()
        a = remote(held.at[y, hrows(n)], held.at[y, hrows(n)], ysend.at[0, n], yrecv.at[0, n], i, y_up)
        b = remote(held.at[y, hrows(n)], held.at[y, hrows(n)], ysend.at[1, n], yrecv.at[1, n], i, y_down)
        a.start()
        b.start()
        up.append(a)
        down.append(b)
        sent.extend([a, b])

    for n in range(min(AHEAD, NC)):
        gather_own(n)

    def gather_relay(n):
        up[n].wait_recv()
        a = remote(held.at[y_down, hrows(n, 0)], held.at[y_down, hrows(n, 0)], ysend.at[2, n], yrecv.at[2, n], i, y_up)
        a.start()
        down[n].wait_recv()
        b = remote(held.at[y_up, hrows(n, 1)], held.at[y_up, hrows(n, 1)], ysend.at[3, n], yrecv.at[3, n], i, y_down)
        b.start()
        sent.extend([a, b])
        if n + AHEAD < NC:
            gather_own(n + AHEAD)
        return a, b

    lane = lax.broadcasted_iota(jnp.int32, (64, LANES), 1)
    low = lane < 64

    def project(n):
        blocks = CHUNKS[n]
        for j in range(blocks):
            base = first_row[n] + j * PACK
            out = slice(j * BLK, (j + 1) * BLK)
            top = slice(j * BLK, j * BLK + 64)
            bot = slice(j * BLK + 64, (j + 1) * BLK)
            for a in range(4):
                lhs[out, a * LANES:(a + 1) * LANES] = held[a, base:base + BLK, :]
            for pair in range(2):
                p0 = held[2 * pair, base + BLK:base + PACK, :]
                p1 = held[2 * pair + 1, base + BLK:base + PACK, :]
                cols = slice(512 + pair * LANES, 512 + (pair + 1) * LANES)
                lhs[top, cols] = jnp.concatenate([p0[:, :64], p1[:, :64]], axis=1)
                lhs[bot, cols] = jnp.concatenate([p0[:, 64:], p1[:, 64:]], axis=1)
        res = jnp.dot(lhs[:blocks * BLK], w_ref[...], preferred_element_type=jnp.float32) + bias
        for j in range(blocks):
            r0 = j * BLK
            base = first_row[n] + j * PACK
            g_ref[4, HEAD + base:HEAD + base + BLK, :] = res[r0:r0 + BLK, :LANES].astype(jnp.bfloat16)
            s_ref[base:base + BLK, :] = res[r0:r0 + BLK, LANES:2 * LANES]
            top = res[r0:r0 + 64, 2 * LANES:]
            bot = res[r0 + 64:r0 + BLK, 2 * LANES:]
            g_ref[4, HEAD + base + BLK:HEAD + base + PACK, :] = jnp.where(
                low, top, pltpu.roll(bot, 64, 1)).astype(jnp.bfloat16)
            s_ref[base + BLK:base + PACK, :] = jnp.where(low, pltpu.roll(top, 64, 1), bot)

    whole_to = x_down + core * (x_up - x_down)
    whole_from, whole_at = 6 - 4 * core, 8 - 8 * core
    list_to = x_up + core * (x_down - x_up)
    list_from, list_at = 2 + 4 * core, 8 * core
    ours, first, second, listed = [], [], [], []

    def group(m):
        size = sum(CHUNKS) // GROUPS * PACK
        return pl.ds(0, HEAD + size) if m == 0 else pl.ds(HEAD + m * size, size)

    def send_own(n):
        src = g_ref.at[4, grows(n)]
        a = remote(src, g_ref.at[2, grows(n)], xsend.at[0, n], xrecv.at[0, n], x_up, y)
        b = remote(src, g_ref.at[6, grows(n)], xsend.at[1, n], xrecv.at[1, n], x_down, y)
        c = remote(src, g_ref.at[3 + 2 * core, grows(n)], psend.at[0, n], precv.at[0, n], partner, y)
        a.start()
        b.start()
        ours.append((a, b, c))
        sent.extend([a, b, c])

    def relay_group(m):
        per = NC // GROUPS
        for n in range(m * per, (m + 1) * per):
            ours[n][0].wait_recv()
            ours[n][1].wait_recv()
        u = remote(g_ref.at[whole_from, group(m)], g_ref.at[whole_at, group(m)], xsend.at[2, m], xrecv.at[2, m], whole_to, y)
        pu = remote(g_ref.at[2, group(m)], g_ref.at[1 + 2 * core, group(m)], psend.at[1, m], precv.at[1, m], partner, y)
        pv = remote(g_ref.at[6, group(m)], g_ref.at[5 + 2 * core, group(m)], psend.at[2, m], precv.at[2, m], partner, y)
        u.start()
        ours[m][2].start()
        if m < GROUPS - 1:
            pu.start()
            pv.start()
        first.append((u, pu, pv))
        sent.extend([u, pu, pv])

    def pick_blocks(low_block, high_block):
        table = g_ref[list_from, :HEAD, :].astype(jnp.float32)
        wanted = jnp.where(core == 1, table[7:8], table[6:7])
        short = lax.broadcasted_iota(jnp.int32, (1, LANES), 1)

        def pick(s, carry):
            block = jnp.sum(jnp.where(short == s, wanted, 0.0), axis=1, keepdims=True)
            block = jnp.broadcast_to(block, (16, LANES))
            place = pl.ds(pl.multiple_of(HEAD + s * PACK, 16), PACK)
            if low_block == 0:
                total = jnp.zeros((PACK // 16, 16, LANES), jnp.bfloat16)
            else:
                total = picked[place, :].reshape(PACK // 16, 16, LANES)
            for j in range(low_block, high_block):
                one = jnp.where(block == float(j), 1.0, 0.0).astype(jnp.bfloat16)
                rows = g_ref[list_from, HEAD + j * PACK:HEAD + (j + 1) * PACK, :]
                total = total + rows.reshape(PACK // 16, 16, LANES) * one[None]
            picked[place, :] = total.reshape(PACK, LANES)
            return carry

        lax.fori_loop(0, SLOTS, pick, 0)

    def relay_list():
        picked[:HEAD, :] = g_ref[list_from, :HEAD, :]
        pick_blocks(sum(CHUNKS[:-1]), sum(CHUNKS))
        copy = remote(picked, g_ref.at[list_at, pl.ds(0, HEAD + SLOTS * PACK)], xsend.at[3, 0], xrecv.at[3, 0], list_to, y)
        copy.start()
        listed.append(copy)
        sent.append(copy)

    def relay_two(m):
        first[m][0].wait_recv()
        c = remote(g_ref.at[whole_at, group(m)], g_ref.at[7 - 6 * core, group(m)], psend.at[3, m], precv.at[3, m], partner, y)
        c.start()
        second.append(c)
        sent.append(c)

    g_ref[PLACES, :PACK, :] = jnp.zeros((PACK, LANES), jnp.bfloat16)
    odd = lax.rem(y, 2) == 1
    for load in raws:
        load.wait()
    n_first, n_rest = cut(raw[0], odd)
    s_first, s_rest = cut(raw[1], odd)
    rest = jnp.concatenate([n_rest, s_rest], axis=1)
    for a in range(4):
        for part, cols in ((n_first, 0), (s_first, 1), (rest, 2)):
            cols = slice(cols * LANES, (cols + 1) * LANES)
            w_ref[a * BLK:(a + 1) * BLK, cols] = part[a * PACK:a * PACK + BLK]
            w_ref[512 + a * 64:512 + (a + 1) * 64, cols] = part[a * PACK + BLK:(a + 1) * PACK]
    b_first, b_rest = cut(b_ref[layer:layer + 1, window], odd)
    bias = jnp.concatenate([jnp.zeros((1, LANES), jnp.float32), b_first, jnp.zeros((1, 64), jnp.float32), b_rest], axis=1)

    tab[...] = jnp.zeros(tab.shape, jnp.float32)
    tab[:PEERS, :SLOTS] = list_ref[...].astype(jnp.float32)
    diagonal = lax.broadcasted_iota(jnp.int32, (PEERS, PEERS), 0) == lax.broadcasted_iota(jnp.int32, (PEERS, PEERS), 1)
    many = jnp.where(diagonal, many_ref[...].astype(jnp.float32), 0.0)
    tab[:PEERS, SLOTS:SLOTS + 1] = jnp.sum(many, axis=1, keepdims=True)
    g_ref[4, :HEAD, :] = tab[...].astype(jnp.bfloat16)

    relays = [gather_relay(0)]
    for n in range(NC):
        for relay in relays[n]:
            relay.wait_recv()
        project(n)
        send_own(n)
        if n + 1 < NC:
            relays.append(gather_relay(n + 1))
        for m in range(GROUPS):
            if n == min((m + 1) * (NC // GROUPS), NC - 1):
                relay_group(m)
                if m == GROUPS - 2:
                    pick_blocks(0, sum(CHUNKS[:-1]))
    relay_list()
    first[-1][1].start()
    first[-1][2].start()
    for m in range(GROUPS):
        relay_two(m)
    for n in range(NC):
        ours[n][2].wait_recv()
    for m in range(GROUPS):
        first[m][1].wait_recv()
        first[m][2].wait_recv()
        second[m].wait_recv()
    listed[0].wait_recv()
    if layer == 0:
        order_tiles(count_ref[0], dst_ref[...], src_ref[...], core, g_ref, idx_ref)
    else:
        idx_ref[...] = jnp.zeros(idx_ref.shape, idx_ref.dtype)
    for copy in sent:
        copy.wait_send()


def aggregate(last, idx, gv, tv, s_ref, out_ref, part):
    lane = lax.broadcasted_iota(jnp.int32, (64, LANES), 1)
    low = lane < 64

    def source(q):
        row = pl.multiple_of(idx[1, q], 16)
        ones = jnp.full((64, 64), idx[2, q].astype(jnp.float32)).astype(jnp.bfloat16)
        left = gv[pl.ds(row, BLK), :]
        pack = gv[pl.ds(row + BLK, 64), :]
        right = jnp.concatenate([
            jnp.concatenate([pack[:, :64], ones], axis=1),
            jnp.concatenate([pack[:, 64:], ones], axis=1),
        ], axis=0)
        return jnp.concatenate([left, right], axis=1)

    def product(p):
        q = 2 * p
        lhs = jnp.concatenate([tv[idx[0, q]], tv[idx[0, q + 1]]], axis=1)
        rhs = jnp.concatenate([source(q), source(q + 1)], axis=0)
        return jnp.dot(lhs, rhs, preferred_element_type=jnp.float32)

    part[0] = jnp.zeros(part.shape[1:], jnp.float32)

    def step(g, carry):
        products = [product(g * UNROLL + u) for u in range(UNROLL)]
        for u in range(UNROLL):
            p = g * UNROLL + u
            part[p + 1] = part[p] * idx[3, p].astype(jnp.float32) + products[u]
        return carry

    lax.fori_loop(0, (part.shape[0] - 1) // UNROLL, step, 0)

    for b in range(s_ref.shape[0] // PACK):
        acc = part[idx[4, b]]
        scale = 1.0 / (1.0 + acc[:, PACK:PACK + 1])
        left = acc[:, :LANES] * scale
        right = acc[:, LANES:] * scale
        pack = jnp.where(low, right[:64], pltpu.roll(right[64:], 64, 1))
        base = b * PACK
        left = left + s_ref[base:base + BLK, :]
        pack = pack + s_ref[base + BLK:base + PACK, :]
        if last:
            row = b * BLK
            out_ref[row:row + BLK, :LANES] = left.astype(jnp.bfloat16)
            out_ref[row:row + 64, LANES:] = pack[:, :64].astype(jnp.bfloat16)
            out_ref[row + 64:row + BLK, LANES:] = pltpu.roll(pack, 64, 1)[:, :64].astype(jnp.bfloat16)
        else:
            out_ref[base:base + BLK, :] = jnp.maximum(left, 0.0).astype(jnp.bfloat16)
            out_ref[base + BLK:base + PACK, :] = jnp.maximum(pack, 0.0).astype(jnp.bfloat16)


def per_device(
    feats, tile_vals, tile_dst, tile_src, tile_count, send_blocks, send_count, w_self, w_nbr, bias
):
    node_rows, cols = feats.shape
    blk_dev = node_rows // BLK
    packed_rows = blk_dev * PACK
    slot_rows = HEAD + packed_rows
    tiles = tile_vals.shape[0]
    entries = tiles + blk_dev

    f3 = feats.reshape(blk_dev, BLK, cols)
    hidden = jnp.concatenate(
        [f3[..., :128], jnp.concatenate([f3[:, :64, 128:], f3[:, 64:, 128:]], axis=2)], axis=1
    ).reshape(packed_rows, LANES)

    NC = len(CHUNKS)
    vmem = pl.BlockSpec(memory_space=pltpu.VMEM)
    anywhere = pl.BlockSpec(memory_space=pl.ANY)
    hbm = pl.BlockSpec(memory_space=pltpu.HBM)

    def exchange_call(layer):
        return pl.pallas_call(
            functools.partial(exchange, layer),
            out_shape=(
                jax.ShapeDtypeStruct((PLACES + 1, slot_rows, LANES), jnp.bfloat16),
                jax.ShapeDtypeStruct((packed_rows, LANES), jnp.float32),
                jax.ShapeDtypeStruct((8, 2 * LANES), jnp.int32),
            ),
            in_specs=[pl.BlockSpec(memory_space=pltpu.SMEM), anywhere, vmem, vmem, hbm, hbm, vmem, vmem, vmem],
            out_specs=(vmem, vmem, vmem),
            scratch_shapes=[
                pltpu.VMEM((4, packed_rows, LANES), jnp.bfloat16),
                pltpu.VMEM((max(CHUNKS) * BLK, 768), jnp.bfloat16),
                pltpu.VMEM((2, 768, 2 * LANES), jnp.bfloat16),
                pltpu.VMEM((768, 3 * LANES), jnp.bfloat16),
                pltpu.VMEM((HEAD + SLOTS * PACK, LANES), jnp.bfloat16),
                pltpu.VMEM((HEAD, LANES), jnp.float32),
                pltpu.SemaphoreType.DMA((NC,)),
                pltpu.SemaphoreType.DMA((2,)),
            ] + [pltpu.SemaphoreType.DMA((4, NC)) for _ in range(6)],
            compiler_params=pltpu.CompilerParams(
                collective_id=layer, has_side_effects=True, vmem_limit_bytes=EXCHANGE_BYTES
            ),
            name=f"exchange{layer}",
        )

    def aggregate_call(last):
        out = (node_rows, cols) if last else (packed_rows, LANES)
        return pl.pallas_call(
            functools.partial(aggregate, last),
            out_shape=jax.ShapeDtypeStruct(out, jnp.bfloat16),
            grid_spec=pltpu.PrefetchScalarGridSpec(
                num_scalar_prefetch=1,
                grid=(),
                in_specs=[vmem, vmem, vmem],
                out_specs=vmem,
                scratch_shapes=[pltpu.VMEM((entries // 2 + 1, BLK, 2 * LANES), jnp.float32)],
            ),
            compiler_params=pltpu.CompilerParams(vmem_limit_bytes=AGGREGATE_BYTES),
            name="aggregate_last" if last else "aggregate",
        )

    dsts, srcs = tile_dst[None, :], tile_src[None, :]
    ws, wn = (pltpu.with_memory_space_constraint(w, pltpu.HBM) for w in (w_self, w_nbr))
    for layer in range(LAYERS):
        g, s, order = exchange_call(layer)(tile_count, hidden, send_blocks[0], send_count, ws, wn, bias, dsts, srcs)
        idx = order if layer == 0 else idx
        g = g.reshape((PLACES + 1) * slot_rows, LANES)
        hidden = aggregate_call(layer == LAYERS - 1)(idx, g, tile_vals, s)
    return hidden


def solution(mesh):
    in_specs = (
        P("dom", "feat"),
        P("dom", None, None),
        P("dom"),
        P("dom"),
        P("dom"),
        P("dom", None, None),
        P("dom", None),
        P(),
        P(),
        P(),
    )
    out_specs = P("dom", "feat")
    return jax.shard_map(
        per_device, mesh=mesh, in_specs=in_specs, out_specs=out_specs, check_vma=False
    )
```
